512 devices in a mesh: rowg: 16 (over y_hi, x, core), colg: 32 (over y_lo, z).
Axes of the slice: x: 4, y: 4 (y_hi: 2, y_lo: 2; y = y_hi * 2 + y_lo), z: 16, core: 2. Of those that a mesh axis runs over, the one named last changes fastest.
Arguments:
- pair_rows: int32 [8192, 32768], P('rowg', 'colg'), may hold values from 0 to 240
- reducers: int32 [2, 1024, 32768], P(None, 'rowg', 'colg'), may hold values from 0 to 240
- pivots: int32 [2, 1024], replicated, may hold values from 0 to 32767, as said below
- counts: int32 [16], replicated, may hold values from 0 to 512, as said below
Outputs:
- reduced: int32 [4096, 32768], P('rowg', 'colg')
The draws below stay inside these ranges and needn't reach their ends.
Inputs may be any that keep to these rules, and one draw needn't show every extreme that they name: `pivots`: the 2048 pivot columns are all different; column 0 and column 32767 are among them. `counts`: owners 2i and 2i + 1 together hold 512 live rows; some owner has exactly 512 live rows and its partner none; owner 16 - 2 holds more than 256 live rows.
All inputs are finite; a program needn't handle non-finite values.
Results may differ from the reference program's by a relative error of at most 0.000001.
Values may be sent and summed in bfloat16 or wider, within the bound.
No kernel may reach another device: no remote copies, remote signals or barrier semaphores. Data moves between devices by JAX's collectives and lax.ppermute only.
A program may use at most 64 MiB of HBM per device.

```python
import jax
import jax.numpy as jnp
from jax import lax

C = 32768
K = 1024
PANELS = 2
LIVE_DEV = 256
CAP = 512
TOTAL = 4096
SLOTS = 8192
OWNERS = 16


def draw_pivots(key, part):
    middle = jax.random.permutation(key, C - 2)[:PANELS * K - 2] + 1
    corners = jnp.array([0, C - 1], jnp.int32)
    chosen = jnp.concatenate([corners, middle.astype(jnp.int32)])
    shuffle = jax.random.permutation(jax.random.fold_in(key, 7), PANELS * K)
    return jnp.take(chosen, shuffle).reshape(PANELS, K).astype(jnp.int32)


def draw_counts(key, part):
    pairs_total = OWNERS // 2
    firsts = jax.random.randint(jax.random.fold_in(key, 11), (pairs_total,), 0, CAP + 1).astype(jnp.int32)
    last_first = jax.random.randint(jax.random.fold_in(key, 19), (), LIVE_DEV + 1, CAP + 1).astype(jnp.int32)
    pair_ids = lax.iota(jnp.int32, pairs_total)
    firsts = jnp.where(pair_ids == pairs_total - 1, last_first, firsts).astype(jnp.int32)
    forced = jax.random.randint(jax.random.fold_in(key, 13), (), 0, pairs_total).astype(jnp.int32)
    side = jax.random.randint(jax.random.fold_in(key, 17), (), 0, 2).astype(jnp.int32)
    side = jnp.where(forced == pairs_total - 1, 1, side).astype(jnp.int32)
    marks = pair_ids == forced
    firsts = jnp.where(marks, side * CAP, firsts).astype(jnp.int32)
    seconds = (CAP - firsts).astype(jnp.int32)
    return jnp.stack([firsts, seconds], axis=1).reshape(OWNERS).astype(jnp.int32)


def plant(drawn, own_key, least, largest):
    shape = drawn.shape
    spot = [jax.random.randint(jax.random.fold_in(own_key, axis), (), 0, shape[axis]) for axis in range(len(shape))]
    drawn = drawn.at[tuple(spot)].set(least)
    longest = shape.index(max(shape))
    spot[longest] = (spot[longest] + 1) % shape[longest]
    return drawn.at[tuple(spot)].set(largest)


def setup_inputs(seed: int = 0) -> dict:
    arg_keys = jax.random.split(jax.random.key(seed), 5)
    return {
        "pair_rows": plant(jax.random.randint(arg_keys[0], (SLOTS, C), 0, 241), jax.random.fold_in(arg_keys[0], 1), 0, 240).astype(jnp.int32),
        "reducers": plant(jax.random.randint(arg_keys[1], (PANELS, K, C), 0, 241), jax.random.fold_in(arg_keys[1], 1), 0, 240).astype(jnp.int32),
        "pivots": draw_pivots(jax.random.fold_in(arg_keys[4], 71), 0),
        "counts": draw_counts(jax.random.fold_in(arg_keys[4], 71), 0),
    }


modulus = 241.0
half_modulus = 120.0


def centered(values):
    return values - modulus * (values > half_modulus).astype(values.dtype)


def normalized(panel, pivot_cols, all_pivots):
    columns = lax.iota(jnp.int32, panel.shape[1])
    is_pivot = jnp.zeros((panel.shape[1],), jnp.int32).at[all_pivots].set(1)
    own_pivot = columns[None, :] == pivot_cols[:, None]
    entries = centered(panel.astype(jnp.float32))
    ones = jnp.ones_like(entries)
    zeros = jnp.zeros_like(entries)
    kept = jnp.where(is_pivot[None, :] > 0, jnp.where(own_pivot, ones, zeros), entries)
    return kept.astype(jnp.bfloat16)


def apply_panel(matrix_rows, normed, pivot_cols):
    picked = jnp.take(matrix_rows, pivot_cols, axis=1)
    factors = centered(picked).astype(jnp.bfloat16)
    product = jnp.dot(factors, normed, preferred_element_type=jnp.float32)
    return jnp.mod(matrix_rows - product, modulus)


def reference(pair_rows, reducers, pivots, counts):
    ends = jnp.cumsum(counts).astype(jnp.int32)
    starts = (ends - counts).astype(jnp.int32)
    rank_ids = lax.iota(jnp.int32, TOTAL)
    owner_ids = jnp.sum((rank_ids[:, None] >= ends[None, :]).astype(jnp.int32), axis=1).astype(jnp.int32)
    owner_start = jnp.take(starts, owner_ids).astype(jnp.int32)
    slot_ids = (owner_ids * CAP + rank_ids - owner_start).astype(jnp.int32)
    matrix_rows = jnp.take(pair_rows, slot_ids, axis=0).astype(jnp.float32)
    all_pivots = pivots.reshape(-1)
    for panel in range(PANELS):
        normed = normalized(reducers[panel], pivots[panel], all_pivots)
        matrix_rows = apply_panel(matrix_rows, normed, pivots[panel])
    return matrix_rows.astype(jnp.int32)
```

```python
import jax
import jax.numpy as jnp
from jax import lax
from jax.sharding import Mesh, PartitionSpec as P

PANELS = 2
LIVE_DEV = 256
CAP = 96

ROW = ("yh", "x", "core")
COL = ("yl", "z")

modulus = 241.0
half_modulus = 120.0


def centered(values):
    return values - modulus * (values > half_modulus).astype(values.dtype)


def pick_value(table, position):
    marks = lax.iota(jnp.int32, table.shape[0]) == position
    return jnp.sum(jnp.where(marks, table, jnp.zeros_like(table)))


def swap(value, axis):
    return lax.ppermute(value, axis, [(0, 1), (1, 0)])


def take_window(source, start, rows):
    index = start + lax.iota(jnp.int32, rows)
    return jnp.take(source, jnp.clip(index, 0, source.shape[0] - 1), axis=0)


def compact_rows(pair_rows, counts):
    row_index = lax.axis_index(ROW)
    second = lax.axis_index("core")
    first_count = pick_value(counts, row_index - second)
    slots = pair_rows.astype(jnp.float32).astype(jnp.bfloat16)
    keep_start = second * (LIVE_DEV - first_count)
    send_start = jnp.where(second == 0, LIVE_DEV, -first_count)
    kept = take_window(slots, keep_start, LIVE_DEV)
    incoming = swap(take_window(slots, send_start, LIVE_DEV), "core")
    place = lax.iota(jnp.int32, LIVE_DEV)
    mine = jnp.where(second == 0, place < first_count, place >= first_count - LIVE_DEV)
    return jnp.where(mine[:, None], kept, incoming)


def normalize_block(block, own_cols, all_pivots, col_start):
    columns = col_start + lax.iota(jnp.int32, block.shape[1])
    is_pivot = jnp.any(columns[:, None] == all_pivots[None, :], axis=1)
    own_pivot = columns[None, :] == own_cols[:, None]
    entries = centered(block.astype(jnp.float32))
    ones = jnp.ones_like(entries)
    zeros = jnp.zeros_like(entries)
    kept = jnp.where(is_pivot[None, :], jnp.where(own_pivot, ones, zeros), entries)
    return kept.astype(jnp.bfloat16)


def shards(pair_rows, reducers, pivots, counts):
    row_index = lax.axis_index(ROW)
    col_index = lax.axis_index(COL)
    lower = lax.axis_index("yl")
    col_width = pair_rows.shape[1]
    col_start = col_index * col_width
    rows_dev = reducers.shape[1]
    order = pivots.reshape(PANELS, -1, rows_dev).transpose(1, 0, 2).reshape(-1)
    total = order.shape[0]
    own_cols = lax.dynamic_slice_in_dim(order, row_index * PANELS * rows_dev, PANELS * rows_dev)
    normed = normalize_block(reducers.reshape(PANELS * rows_dev, col_width), own_cols, order, col_start)
    panel = lax.all_gather(normed, ROW, axis=0, tiled=True)

    live = compact_rows(pair_rows, counts)

    owner = order // col_width
    ids = lax.iota(jnp.int32, total)
    same = owner[:, None] == owner[None, :]
    rank = jnp.sum((same & (ids[None, :] < ids[:, None])).astype(jnp.int32), axis=1)
    rounds = jnp.max(rank) // CAP + 1
    z_size = lax.axis_size("z")
    slot = (owner % z_size) * (2 * CAP) + (owner // z_size) * CAP

    def fetch(step):
        base = step * CAP
        want = base + lax.iota(jnp.int32, CAP)
        hit = (owner == col_index)[None, :] & (rank[None, :] == want[:, None])
        local = jnp.sum(jnp.where(hit, order[None, :] - col_start + 1, 0), axis=1) - 1
        choose = (local[:, None] == lax.iota(jnp.int32, col_width)[None, :]).astype(jnp.bfloat16)
        mine = lax.dot_general(choose, live, (((1,), (1,)), ((), ())), preferred_element_type=jnp.float32)
        mine = centered(mine).astype(jnp.bfloat16)
        theirs = swap(mine, "yl")
        both = jnp.where(lower == 0, jnp.stack([mine, theirs]), jnp.stack([theirs, mine]))
        spread = lax.all_gather(both.reshape(2 * CAP, LIVE_DEV), "z", axis=0, tiled=True)
        inside = (rank >= base) & (rank < base + CAP)
        got = jnp.take(spread, jnp.where(inside, slot + rank - base, 0), axis=0)
        return jnp.where(inside[:, None], got, jnp.zeros_like(got))

    half = total // 2

    def reduce_by(result, factors):
        for part in range(2):
            product = lax.dot_general(
                factors[part * half:(part + 1) * half],
                panel[part * half:(part + 1) * half],
                (((0,), (0,)), ((), ())),
                preferred_element_type=jnp.float32,
            )
            result = jnp.mod(result - product, modulus)
        return result

    first = reduce_by(live.astype(jnp.float32), fetch(0)).astype(jnp.int32)
    _, result = lax.while_loop(
        lambda state: state[0] < rounds,
        lambda state: (
            state[0] + 1,
            reduce_by(state[1].astype(jnp.float32), fetch(state[0])).astype(jnp.int32),
        ),
        (jnp.int32(1), first),
    )
    return result


def solution(mesh):
    fine = Mesh(mesh.devices.reshape(2, 4, 2, 2, 16), (*ROW, *COL))
    return jax.shard_map(
        shards,
        mesh=fine,
        in_specs=(P(ROW, COL), P(None, ROW, COL), P(), P()),
        out_specs=P(ROW, COL),
        check_vma=False,
    )
```

```python
import jax
import jax.numpy as jnp
from jax import lax
from jax.sharding import Mesh, PartitionSpec as P


PANELS = 2
LIVE_DEV = 256
CAP = 96

ROW = ("yh", "x", "core")
COL = ("yl", "z")
CHIP = ("yh", "x")

modulus = 241.0
half_modulus = 120.0


def centered(values):
    return values - modulus * (values > half_modulus).astype(values.dtype)


def pick_value(table, position):
    marks = lax.iota(jnp.int32, table.shape[0]) == position
    return jnp.sum(jnp.where(marks, table, jnp.zeros_like(table)))


def swap(value, axis):
    return lax.ppermute(value, axis, [(0, 1), (1, 0)])


def take_window(source, start, rows):
    index = start + lax.iota(jnp.int32, rows)
    return jnp.take(source, jnp.clip(index, 0, source.shape[0] - 1), axis=0)


def compact_rows(pair_rows, counts):
    row_index = lax.axis_index(ROW)
    second = lax.axis_index("core")
    first_count = pick_value(counts, row_index - second)
    slots = pair_rows.astype(jnp.float32).astype(jnp.bfloat16)
    keep_start = second * (LIVE_DEV - first_count)
    send_start = jnp.where(second == 0, LIVE_DEV, -first_count)
    kept = take_window(slots, keep_start, LIVE_DEV)
    incoming = swap(take_window(slots, send_start, LIVE_DEV), "core")
    place = lax.iota(jnp.int32, LIVE_DEV)
    mine = jnp.where(second == 0, place < first_count, place >= first_count - LIVE_DEV)
    return jnp.where(mine[:, None], kept, incoming)


def normalize_block(block, own_cols, all_pivots, col_start):
    columns = col_start + lax.iota(jnp.int32, block.shape[1])
    is_pivot = jnp.any(columns[:, None] == all_pivots[None, :], axis=1)
    own_pivot = columns[None, :] == own_cols[:, None]
    entries = centered(block.astype(jnp.float32))
    ones = jnp.ones_like(entries)
    zeros = jnp.zeros_like(entries)
    kept = jnp.where(is_pivot[None, :], jnp.where(own_pivot, ones, zeros), entries)
    return kept.astype(jnp.bfloat16)


def shards(pair_rows, reducers, pivots, counts):
    col_index = lax.axis_index(COL)
    lower = lax.axis_index("yl")
    core = lax.axis_index("core")
    chip = lax.axis_index(CHIP)
    chips = lax.axis_size(CHIP)
    col_width = pair_rows.shape[1]
    col_start = col_index * col_width
    rows_dev = PANELS * reducers.shape[1]
    order = pivots.reshape(PANELS, chips, 2, -1).transpose(2, 1, 0, 3).reshape(-1)
    total = order.shape[0]
    half = total // 2
    own_cols = lax.dynamic_slice_in_dim(order, core * half + chip * rows_dev, rows_dev)
    normed = normalize_block(reducers.reshape(rows_dev, col_width), own_cols, order, col_start)
    copies = jnp.broadcast_to(normed[None], (chips, rows_dev, col_width))
    mine_panel = lax.all_to_all(copies, CHIP, 0, 0, tiled=True).reshape(half, col_width)
    panels = (mine_panel, swap(mine_panel, "core"))

    live = compact_rows(pair_rows, counts)

    owner = order // col_width
    ids = lax.iota(jnp.int32, total)
    same = owner[:, None] == owner[None, :]
    rank = jnp.sum((same & (ids[None, :] < ids[:, None])).astype(jnp.int32), axis=1)
    rounds = jnp.max(rank) // CAP + 1
    z_size = lax.axis_size("z")
    slot = (owner % z_size) * (2 * CAP) + (owner // z_size) * CAP + rank
    pairs = jnp.stack([rank, slot]).reshape(2, 2, half)
    pairs = jnp.where(core == 0, pairs, pairs[:, ::-1])
    my_rank, my_slot = pairs.reshape(2, total)

    def fetch(step):
        base = step * CAP
        want = base + lax.iota(jnp.int32, CAP)
        hit = (owner == col_index)[None, :] & (rank[None, :] == want[:, None])
        local = jnp.sum(jnp.where(hit, order[None, :] - col_start + 1, 0), axis=1) - 1
        choose = (local[:, None] == lax.iota(jnp.int32, col_width)[None, :]).astype(jnp.bfloat16)
        mine = lax.dot_general(choose, live, (((1,), (1,)), ((), ())), preferred_element_type=jnp.float32)
        mine = centered(mine).astype(jnp.int16)
        theirs = swap(mine, "yl")
        both = jnp.where(lower == 0, jnp.stack([mine, theirs]), jnp.stack([theirs, mine]))
        spread = lax.all_gather(both.reshape(2 * CAP, LIVE_DEV), "z", axis=0, tiled=True)
        spread = spread.astype(jnp.bfloat16)
        inside = (my_rank >= base) & (my_rank < base + CAP)
        got = jnp.take(spread, jnp.where(inside, my_slot - base, 0), axis=0)
        return jnp.where(inside[:, None], got, jnp.zeros_like(got))

    def reduce_by(result, factors):
        for part in range(2):
            product = lax.dot_general(
                factors[part * half:(part + 1) * half],
                panels[part],
                (((0,), (0,)), ((), ())),
                preferred_element_type=jnp.float32,
            )
            result = jnp.mod(result - product, modulus)
        return result

    factors = fetch(0)
    first = reduce_by(live.astype(jnp.float32), factors).astype(jnp.int32)
    _, result = lax.while_loop(
        lambda state: state[0] < rounds,
        lambda state: (
            state[0] + 1,
            reduce_by(state[1].astype(jnp.float32), fetch(state[0])).astype(jnp.int32),
        ),
        (jnp.int32(1), first),
    )
    return result


def solution(mesh):
    fine = Mesh(mesh.devices.reshape(2, 4, 2, 2, 16), (*ROW, *COL))
    return jax.shard_map(
        shards,
        mesh=fine,
        in_specs=(P(ROW, COL), P(None, ROW, COL), P(), P()),
        out_specs=P(ROW, COL),
        check_vma=False,
    )
```

```python
import jax
import jax.numpy as jnp
from jax import lax
from jax.experimental import pallas as pl
from jax.experimental.pallas import tpu as pltpu
from jax.sharding import Mesh, PartitionSpec as P


PANELS = 2
LIVE_DEV = 256
CAP = 96
LANES = 128

ROW = ("yh", "x", "core")
COL = ("yl", "z")
CHIP = ("yh", "x")

modulus = 241.0
half_modulus = 120.0

NN = (((1,), (0,)), ((), ()))
NT = (((1,), (1,)), ((), ()))


def centered(values):
    return values - modulus * (values > half_modulus).astype(values.dtype)


def remainder(values):
    rest = values - modulus * jnp.floor(values * (1.0 / modulus))
    rest = jnp.where(rest < 0.0, rest + modulus, rest)
    return jnp.where(rest >= modulus, rest - modulus, rest)


def swap(value, axis):
    return lax.ppermute(value, axis, [(0, 1), (1, 0)])


def dot(left, right, dims):
    return lax.dot_general(left, right, dims, preferred_element_type=jnp.float32)


def spread_row(grid):
    return jnp.concatenate([grid[i:i + 1] for i in range(grid.shape[0])], axis=1)


def front_kernel(counts, pivots, rows, reducers, normed, kept, sent, slots):
    width = rows.shape[1]
    groups = width // LANES
    core = lax.axis_index("core")
    owner = (lax.axis_index("yh") * 4 + lax.axis_index("x")) * 2 + core
    start = (lax.axis_index("yl") * 16 + lax.axis_index("z")) * width

    count = pivots.shape[1]
    lane_rows = lax.broadcasted_iota(jnp.int32, (LANES, count), 0)
    group_rows = lax.broadcasted_iota(jnp.int32, (groups, count), 0)
    marks = jnp.zeros((groups, LANES), jnp.float32)
    for panel in range(PANELS):
        place = pivots[panel:panel + 1, :] - start
        high = jnp.where((place >= 0) & (place < width), place >> 7, -1)
        marks += dot(
            (group_rows == high).astype(jnp.float32).astype(jnp.bfloat16),
            (lane_rows == (place & (LANES - 1))).astype(jnp.float32).astype(jnp.bfloat16),
            NT,
        )
    flags = marks.astype(jnp.bfloat16)
    lower = lax.broadcasted_iota(jnp.int32, (LANES, LANES), 0)
    upper = lax.broadcasted_iota(jnp.int32, (LANES, LANES), 1)
    inside = dot(flags, (lower < upper).astype(jnp.float32).astype(jnp.bfloat16), NN)
    totals = dot(flags, jnp.ones((LANES, LANES), jnp.bfloat16), NN)
    before = jnp.zeros((groups, LANES), jnp.float32)
    group_ids = lax.broadcasted_iota(jnp.int32, (groups, LANES), 0)
    for group in range(groups - 1):
        before += jnp.where(group_ids > group, totals[group:group + 1], 0.0)
    slots[...] = spread_row(jnp.where(marks > 0.0, inside + before, -1.0))

    rows_dev = reducers.shape[0]
    part = rows_dev // PANELS
    own = pivots[:, pl.ds(pl.multiple_of((owner // 2) * LANES, LANES), LANES)].astype(jnp.float32)
    row_ids = lax.broadcasted_iota(jnp.int32, (rows_dev, LANES), 0)
    lane_ids = lax.broadcasted_iota(jnp.int32, (rows_dev, LANES), 1)
    chosen = jnp.where(row_ids < part, own[0:1], own[1:2])
    target = (row_ids & (part - 1)) + part * core
    own_pivot = jnp.sum(jnp.where(lane_ids == target, chosen, 0.0), axis=1, keepdims=True)
    base = start.astype(jnp.float32)
    for group in range(groups):
        cols = slice(group * LANES, (group + 1) * LANES)
        here = (lane_ids + group * LANES).astype(jnp.float32) + base
        entries = centered(reducers[:, cols].astype(jnp.float32))
        pivot_value = jnp.where(here == own_pivot, 1.0, 0.0)
        normed[:, cols] = jnp.where(marks[group:group + 1] > 0.0, pivot_value, entries).astype(jnp.bfloat16)

    first = counts[owner - core]
    mine = counts[owner]
    capacity = rows.shape[0]
    values = rows[...].astype(jnp.float32).astype(jnp.bfloat16)
    slot_ids = lax.broadcasted_iota(jnp.int32, (LIVE_DEV, capacity), 1)
    places = lax.broadcasted_iota(jnp.int32, (LIVE_DEV, capacity), 0)
    live = slot_ids < mine
    for offset, out in ((core * (LIVE_DEV - first), kept), (jnp.where(core == 0, LIVE_DEV, -first), sent)):
        pick = (live & (slot_ids == places + offset)).astype(jnp.float32).astype(jnp.bfloat16)
        out[...] = dot(pick, values, NN).astype(jnp.bfloat16)


def extract_kernel(base, slots, kept, incoming, live, packed):
    width = kept.shape[1]
    values = (kept[...].astype(jnp.float32) + incoming[...].astype(jnp.float32)).astype(jnp.bfloat16)
    live[...] = values
    want = (lax.broadcasted_iota(jnp.int32, (CAP, width), 0) + base[0]).astype(jnp.float32)
    choose = (slots[...] == want).astype(jnp.float32).astype(jnp.bfloat16)
    packed[...] = centered(dot(choose, values, NT)).astype(jnp.int32).astype(jnp.int16)


VMEM = pl.BlockSpec(memory_space=pltpu.VMEM)
SMEM = pl.BlockSpec(memory_space=pltpu.SMEM)


def front(counts, pivots, rows, reducers):
    width = rows.shape[1]
    return pl.pallas_call(
        front_kernel,
        out_shape=(
            jax.ShapeDtypeStruct(reducers.shape, jnp.bfloat16),
            jax.ShapeDtypeStruct((LIVE_DEV, width), jnp.bfloat16),
            jax.ShapeDtypeStruct((LIVE_DEV, width), jnp.bfloat16),
            jax.ShapeDtypeStruct((1, width), jnp.float32),
        ),
        in_specs=[SMEM, VMEM, VMEM, VMEM],
        out_specs=(VMEM,) * 4,
        name="front",
    )(counts, pivots, rows, reducers)


def extract(base, slots, kept, incoming):
    return pl.pallas_call(
        extract_kernel,
        out_shape=(
            jax.ShapeDtypeStruct(kept.shape, jnp.bfloat16),
            jax.ShapeDtypeStruct((CAP, LIVE_DEV), jnp.int16),
        ),
        in_specs=[SMEM, VMEM, VMEM, VMEM],
        out_specs=(VMEM,) * 2,
        name="extract",
    )(base, slots, kept, incoming)


def shards(pair_rows, reducers, pivots, counts):
    lower = lax.axis_index("yl")
    core = lax.axis_index("core")
    chips = lax.axis_size(CHIP)
    z_size = lax.axis_size("z")
    col_width = pair_rows.shape[1]
    rows_dev = PANELS * reducers.shape[1]
    normed, kept, sent, slots = front(counts, pivots, pair_rows, reducers.reshape(rows_dev, col_width))
    incoming = swap(sent, "core")

    order = pivots.reshape(PANELS, chips, 2, -1).transpose(2, 1, 0, 3).reshape(-1)
    total = order.shape[0]
    half = total // 2
    copies = jnp.broadcast_to(normed[None], (chips, rows_dev, col_width))
    mine_panel = lax.all_to_all(copies, CHIP, 0, 0, tiled=True).reshape(half, col_width)
    panels = (mine_panel, swap(mine_panel, "core"))

    owner = order // col_width
    same = owner[:, None] == owner[None, :]
    rank = jnp.sum((same & (order[None, :] < order[:, None])).astype(jnp.int32), axis=1)
    rounds = jnp.max(rank) // CAP + 1
    slot = (owner % z_size) * (2 * CAP) + (owner // z_size) * CAP + rank
    pairs = jnp.stack([rank, slot]).reshape(2, 2, half)
    pairs = jnp.where(core == 0, pairs, pairs[:, ::-1])
    my_rank, my_slot = pairs.reshape(2, total)

    def fetch(step, kept, incoming):
        base = step * CAP
        live, mine = extract(base.reshape(1), slots, kept, incoming)
        theirs = swap(mine, "yl")
        both = jnp.where(lower == 0, jnp.stack([mine, theirs]), jnp.stack([theirs, mine]))
        spread = lax.all_gather(both.reshape(2 * CAP, LIVE_DEV), "z", axis=0, tiled=True)
        here = jnp.where((my_rank >= base) & (my_rank < base + CAP), my_slot - base, -1)
        table = (here[:, None] == lax.iota(jnp.int32, spread.shape[0])[None, :]).astype(jnp.bfloat16)
        factors = dot(table, spread.astype(jnp.bfloat16), NN)
        return live, factors.astype(jnp.bfloat16)

    def reduce_by(result, factors):
        for part in range(2):
            product = dot(factors[part * half:(part + 1) * half], panels[part], (((0,), (0,)), ((), ())))
            result = remainder(result - product)
        return result

    live, factors = fetch(jnp.int32(0), kept, incoming)
    first = reduce_by(live.astype(jnp.float32), factors).astype(jnp.int32)

    def another(state):
        step, result = state
        _, factors = fetch(step, kept, incoming)
        return step + 1, reduce_by(result.astype(jnp.float32), factors).astype(jnp.int32)

    _, result = lax.while_loop(lambda state: state[0] < rounds, another, (jnp.int32(1), first))
    return result


def solution(mesh):
    fine = Mesh(mesh.devices.reshape(2, 4, 2, 2, 16), (*ROW, *COL))
    return jax.shard_map(
        shards,
        mesh=fine,
        in_specs=(P(ROW, COL), P(None, ROW, COL), P(), P()),
        out_specs=P(ROW, COL),
        check_vma=False,
    )
```

```python
import jax
import jax.numpy as jnp
from jax import lax
from jax.experimental import pallas as pl
from jax.experimental.pallas import tpu as pltpu
from jax.sharding import Mesh, PartitionSpec as P


PANELS = 2
LIVE_DEV = 256
CAP = 96
LANES = 128

ROW = ("yh", "x", "core")
COL = ("yl", "z")
CHIP = ("yh", "x")

modulus = 241.0
half_modulus = 120.0

NN = (((1,), (0,)), ((), ()))
NT = (((1,), (1,)), ((), ()))


def centered(values):
    return values - modulus * (values > half_modulus).astype(values.dtype)


def remainder(values):
    rest = values - modulus * jnp.floor(values * (1.0 / modulus))
    rest = jnp.where(rest < 0.0, rest + modulus, rest)
    return jnp.where(rest >= modulus, rest - modulus, rest)


def swap(value, axis):
    return lax.ppermute(value, axis, [(0, 1), (1, 0)])


def dot(left, right, dims):
    return lax.dot_general(left, right, dims, preferred_element_type=jnp.float32)


def spread_row(grid):
    return jnp.concatenate([grid[i:i + 1] for i in range(grid.shape[0])], axis=1)


def front_kernel(counts, pivots, rows, reducers, copies, kept, sent, slots, normed, done):
    width = rows.shape[1]
    groups = width // LANES
    core = lax.axis_index("core")
    owner = (lax.axis_index("yh") * 4 + lax.axis_index("x")) * 2 + core
    start = (lax.axis_index("yl") * 16 + lax.axis_index("z")) * width

    count = pivots.shape[1]
    lane_rows = lax.broadcasted_iota(jnp.int32, (LANES, count), 0)
    group_rows = lax.broadcasted_iota(jnp.int32, (groups, count), 0)
    marks = jnp.zeros((groups, LANES), jnp.float32)
    for panel in range(PANELS):
        place = pivots[panel:panel + 1, :] - start
        high = jnp.where((place >= 0) & (place < width), place >> 7, -1)
        marks += dot(
            (group_rows == high).astype(jnp.float32).astype(jnp.bfloat16),
            (lane_rows == (place & (LANES - 1))).astype(jnp.float32).astype(jnp.bfloat16),
            NT,
        )
    flags = marks.astype(jnp.bfloat16)
    lower = lax.broadcasted_iota(jnp.int32, (LANES, LANES), 0)
    upper = lax.broadcasted_iota(jnp.int32, (LANES, LANES), 1)
    inside = dot(flags, (lower < upper).astype(jnp.float32).astype(jnp.bfloat16), NN)
    totals = dot(flags, jnp.ones((LANES, LANES), jnp.bfloat16), NN)
    before = jnp.zeros((groups, LANES), jnp.float32)
    group_ids = lax.broadcasted_iota(jnp.int32, (groups, LANES), 0)
    for group in range(groups - 1):
        before += jnp.where(group_ids > group, totals[group:group + 1], 0.0)
    slots[...] = spread_row(jnp.where(marks > 0.0, inside + before, -1.0))

    rows_dev = reducers.shape[0]
    part = rows_dev // PANELS
    own = pivots[:, pl.ds(pl.multiple_of((owner // 2) * LANES, LANES), LANES)].astype(jnp.float32)
    row_ids = lax.broadcasted_iota(jnp.int32, (rows_dev, LANES), 0)
    lane_ids = lax.broadcasted_iota(jnp.int32, (rows_dev, LANES), 1)
    chosen = jnp.where(row_ids < part, own[0:1], own[1:2])
    target = (row_ids & (part - 1)) + part * core
    own_pivot = jnp.sum(jnp.where(lane_ids == target, chosen, 0.0), axis=1, keepdims=True)
    base = start.astype(jnp.float32)
    for group in range(groups):
        cols = slice(group * LANES, (group + 1) * LANES)
        here = (lane_ids + group * LANES).astype(jnp.float32) + base
        entries = centered(reducers[:, cols].astype(jnp.float32))
        pivot_value = jnp.where(here == own_pivot, 1.0, 0.0)
        normed[:, cols] = jnp.where(marks[group:group + 1] > 0.0, pivot_value, entries).astype(jnp.bfloat16)
    writes = [pltpu.make_async_copy(normed, copies.at[chip], done.at[chip]) for chip in range(copies.shape[0])]
    for write in writes:
        write.start()

    first = counts[owner - core]
    mine = counts[owner]
    capacity = rows.shape[0]
    values = rows[...].astype(jnp.float32).astype(jnp.bfloat16)
    slot_ids = lax.broadcasted_iota(jnp.int32, (LIVE_DEV, capacity), 1)
    places = lax.broadcasted_iota(jnp.int32, (LIVE_DEV, capacity), 0)
    live = slot_ids < mine
    for offset, out in ((core * (LIVE_DEV - first), kept), (jnp.where(core == 0, LIVE_DEV, -first), sent)):
        pick = (live & (slot_ids == places + offset)).astype(jnp.float32).astype(jnp.bfloat16)
        out[...] = dot(pick, values, NN).astype(jnp.bfloat16)
    for write in writes:
        write.wait()


def ranks_kernel(pivots, ranks, slots, most):
    core = lax.axis_index("core")
    count = pivots.shape[1]
    chunks = 32768 // LANES
    lane_rows = lax.broadcasted_iota(jnp.int32, (LANES, count), 0)
    chunk_rows = lax.broadcasted_iota(jnp.int32, (chunks, count), 0)
    marks = jnp.zeros((chunks, LANES), jnp.float32)
    chunk_marks, lane_marks = [], []
    for panel in range(PANELS):
        place = pivots[panel:panel + 1, :]
        chunk_marks.append((chunk_rows == (place >> 7)).astype(jnp.float32).astype(jnp.bfloat16))
        lane_marks.append(lane_rows == (place & (LANES - 1)))
        marks += dot(chunk_marks[-1], lane_marks[-1].astype(jnp.float32).astype(jnp.bfloat16), NT)
    flags = marks.astype(jnp.bfloat16)
    lower = lax.broadcasted_iota(jnp.int32, (LANES, LANES), 0)
    upper = lax.broadcasted_iota(jnp.int32, (LANES, LANES), 1)
    inside = dot(flags, (lower < upper).astype(jnp.float32).astype(jnp.bfloat16), NN)
    totals = dot(flags, jnp.ones((LANES, LANES), jnp.bfloat16), NN)
    here = lax.broadcasted_iota(jnp.int32, (chunks, chunks), 0)
    other = lax.broadcasted_iota(jnp.int32, (chunks, chunks), 1)
    earlier = (((here >> 3) == (other >> 3)) & (other < here)).astype(jnp.float32).astype(jnp.bfloat16)
    table = inside + dot(earlier, totals.astype(jnp.bfloat16), NN)
    most[0] = jnp.max(jnp.where(marks > 0.0, table, 0.0)).astype(jnp.int32)
    high = jnp.floor(table * (1.0 / 128.0))
    low = (table - 128.0 * high).astype(jnp.bfloat16)
    high = high.astype(jnp.bfloat16)
    first_dims = (((0,), (0,)), ((), ()))
    grids = []
    for panel in range(PANELS):
        found = 128.0 * dot(high, chunk_marks[panel], first_dims) + dot(low, chunk_marks[panel], first_dims)
        rank = jnp.sum(jnp.where(lane_marks[panel], found, 0.0), axis=0, keepdims=True).astype(jnp.int32)
        block = pivots[panel:panel + 1, :] >> 10
        slot = (block & 15) * (2 * CAP) + (block >> 4) * CAP + rank
        for value in (rank, slot):
            grids.append(jnp.concatenate([value[:, i * LANES:(i + 1) * LANES] for i in range(count // LANES)], axis=0))
    left = lax.broadcasted_iota(jnp.int32, grids[0].shape, 1) < LANES // 2
    for out, a, b in ((ranks, grids[0], grids[2]), (slots, grids[1], grids[3])):
        firsts = jnp.where(left, a, pltpu.roll(b, LANES // 2, axis=1))
        seconds = jnp.where(left, pltpu.roll(a, LANES // 2, axis=1), b)
        out[0] = jnp.where(core == 0, firsts, seconds)
        out[1] = jnp.where(core == 0, seconds, firsts)


def extract_kernel(slots, kept, incoming, live, packed):
    width = kept.shape[1]
    values = (kept[...].astype(jnp.float32) + incoming[...].astype(jnp.float32)).astype(jnp.bfloat16)
    live[...] = values
    want = lax.broadcasted_iota(jnp.int32, (CAP, width), 0).astype(jnp.float32)
    choose = (slots[...] == want).astype(jnp.float32).astype(jnp.bfloat16)
    packed[...] = centered(dot(choose, values, NT)).astype(jnp.int32).astype(jnp.int16)


VMEM = pl.BlockSpec(memory_space=pltpu.VMEM)
SMEM = pl.BlockSpec(memory_space=pltpu.SMEM)


def front(counts, pivots, rows, reducers, chips):
    width = rows.shape[1]
    return pl.pallas_call(
        front_kernel,
        out_shape=(
            jax.ShapeDtypeStruct((chips, *reducers.shape), jnp.bfloat16),
            jax.ShapeDtypeStruct((LIVE_DEV, width), jnp.bfloat16),
            jax.ShapeDtypeStruct((LIVE_DEV, width), jnp.bfloat16),
            jax.ShapeDtypeStruct((1, width), jnp.float32),
        ),
        in_specs=[SMEM, VMEM, VMEM, VMEM],
        out_specs=(pl.BlockSpec(memory_space=pl.ANY), VMEM, VMEM, VMEM),
        scratch_shapes=[pltpu.VMEM(reducers.shape, jnp.bfloat16), pltpu.SemaphoreType.DMA((chips,))],
        name="front",
    )(counts, pivots, rows, reducers)


def ranks(pivots):
    grid = jax.ShapeDtypeStruct((2, pivots.shape[1] // LANES, LANES), jnp.int32)
    return pl.pallas_call(
        ranks_kernel,
        out_shape=(grid, grid, jax.ShapeDtypeStruct((1,), jnp.int32)),
        in_specs=[VMEM],
        out_specs=(VMEM, VMEM, SMEM),
        name="ranks",
        compiler_params=pltpu.CompilerParams(vmem_limit_bytes=16 << 20),
        cost_estimate=pl.CostEstimate(flops=2_000_000_000, bytes_accessed=1_000_000, transcendentals=0),
    )(pivots)


def extract(slots, kept, incoming):
    return pl.pallas_call(
        extract_kernel,
        out_shape=(
            jax.ShapeDtypeStruct(kept.shape, jnp.bfloat16),
            jax.ShapeDtypeStruct((CAP, LIVE_DEV), jnp.int16),
        ),
        in_specs=[VMEM, VMEM, VMEM],
        out_specs=(VMEM,) * 2,
        name="extract",
        compiler_params=pltpu.CompilerParams(vmem_limit_bytes=16 << 20),
    )(slots, kept, incoming)


def shards(pair_rows, reducers, pivots, counts):
    lower = lax.axis_index("yl")
    chips = lax.axis_size(CHIP)
    col_width = pair_rows.shape[1]
    rows_dev = PANELS * reducers.shape[1]
    half = chips * rows_dev
    copies, kept, sent, slots = front(counts, pivots, pair_rows, reducers.reshape(rows_dev, col_width), chips)
    incoming = swap(sent, "core")
    my_rank, my_slot, most = ranks(pivots)
    live, mine = extract(slots, kept, incoming)
    my_rank, my_slot = my_rank.reshape(-1), my_slot.reshape(-1)
    rounds = most[0] // CAP + 1

    def gather(mine, base):
        theirs = swap(mine, "yl")
        both = jnp.where(lower == 0, jnp.stack([mine, theirs]), jnp.stack([theirs, mine]))
        spread = lax.all_gather(both.reshape(2 * CAP, LIVE_DEV), "z", axis=0, tiled=True)
        here = jnp.where((my_rank >= base) & (my_rank < base + CAP), my_slot - base, -1)
        table = (here[:, None] == lax.iota(jnp.int32, spread.shape[0])[None, :]).astype(jnp.bfloat16)
        factors = dot(table, spread.astype(jnp.bfloat16), NN)
        return factors.astype(jnp.bfloat16)

    mine_panel = lax.all_to_all(copies, CHIP, 0, 0, tiled=True).reshape(half, col_width)
    factors = gather(mine, 0)
    panels = (mine_panel, swap(mine_panel, "core"))

    def reduce_by(result, factors):
        for part in range(2):
            product = dot(factors[part * half:(part + 1) * half], panels[part], (((0,), (0,)), ((), ())))
            result = remainder(result - product)
        return result

    first = reduce_by(live.astype(jnp.float32), factors).astype(jnp.int32)

    def another(state):
        step, result = state
        base = step * CAP
        want = (lax.iota(jnp.int32, CAP) + base).astype(jnp.float32)
        choose = (slots == want[:, None]).astype(jnp.bfloat16)
        more = centered(dot(choose, live, NT)).astype(jnp.int16)
        return step + 1, reduce_by(result.astype(jnp.float32), gather(more, base)).astype(jnp.int32)

    _, result = lax.while_loop(lambda state: state[0] < rounds, another, (jnp.int32(1), first))
    return result


def solution(mesh):
    fine = Mesh(mesh.devices.reshape(2, 4, 2, 2, 16), (*ROW, *COL))
    return jax.shard_map(
        shards,
        mesh=fine,
        in_specs=(P(ROW, COL), P(None, ROW, COL), P(), P()),
        out_specs=P(ROW, COL),
        check_vma=False,
    )
```

```python
import jax
import jax.numpy as jnp
from jax import lax
from jax.experimental import pallas as pl
from jax.experimental.pallas import tpu as pltpu
from jax.sharding import Mesh, PartitionSpec as P


PANELS = 2
LIVE_DEV = 256
CAP = 96
LANES = 128

ROW = ("yh", "x", "core")
COL = ("yl", "z")
CHIP = ("yh", "x")

modulus = 241.0
half_modulus = 120.0

NN = (((1,), (0,)), ((), ()))
NT = (((1,), (1,)), ((), ()))
TN = (((0,), (0,)), ((), ()))


def centered(values):
    return values - modulus * (values > half_modulus).astype(values.dtype)


def remainder(values):
    rest = values - modulus * jnp.floor(values * (1.0 / modulus))
    rest = jnp.where(rest < 0.0, rest + modulus, rest)
    return jnp.where(rest >= modulus, rest - modulus, rest)


def swap(value, axis):
    return lax.ppermute(value, axis, [(0, 1), (1, 0)])


def dot(left, right, dims):
    return lax.dot_general(left, right, dims, preferred_element_type=jnp.float32)


def spread_row(grid):
    return jnp.concatenate([grid[i:i + 1] for i in range(grid.shape[0])], axis=1)


def one_hot(hits):
    return hits.astype(jnp.float32).astype(jnp.bfloat16)


def strictly_before(size):
    lower = lax.broadcasted_iota(jnp.int32, (size, size), 0)
    upper = lax.broadcasted_iota(jnp.int32, (size, size), 1)
    return one_hot(lower < upper)


def front_kernel(counts, pivots, rows, reducers, copies, placed, keep, send, slots, normed, done):
    width = rows.shape[1]
    capacity = rows.shape[0]
    groups = width // LANES
    core = lax.axis_index("core")
    upper = lax.axis_index("yl")
    depth = lax.axis_index("z")
    owner = (lax.axis_index("yh") * 4 + lax.axis_index("x")) * 2 + core
    start = (upper * 16 + depth) * width

    count = pivots.shape[1]
    lane_rows = lax.broadcasted_iota(jnp.int32, (LANES, count), 0)
    group_rows = lax.broadcasted_iota(jnp.int32, (2 * groups, count), 0)
    side = (lax.broadcasted_iota(jnp.int32, (1, count), 1) >> 6) & 1
    marks = jnp.zeros((2 * groups, LANES), jnp.float32)
    ahead = [jnp.zeros((1, 1), jnp.float32)] * 2
    for panel in range(PANELS):
        pivot = pivots[panel:panel + 1, :]
        place = pivot - start
        high = jnp.where((place >= 0) & (place < width), (place >> 7) + side * groups, -1)
        marks += dot(one_hot(group_rows == high), one_hot(lane_rows == (place & (LANES - 1))), NT)
        for half in range(2):
            first_block = ((pivot >> 10) == depth) & (side == half)
            ahead[half] += jnp.sum(first_block.astype(jnp.float32), axis=1, keepdims=True)
    flags = marks.astype(jnp.bfloat16)
    inside = dot(flags, strictly_before(LANES), NN)
    totals = dot(flags, jnp.ones((LANES, LANES), jnp.bfloat16), NN)
    group_ids = lax.broadcasted_iota(jnp.int32, (groups, LANES), 0)
    columns = []
    for half in range(2):
        part = slice(half * groups, (half + 1) * groups)
        place = inside[part] + jnp.where(upper == 0, 0.0, ahead[half])
        for group in range(groups - 1):
            place += jnp.where(group_ids > group, totals[half * groups + group:half * groups + group + 1], 0.0)
        columns.append(spread_row(jnp.where(marks[part] > 0.0, place, -1.0)))
        slots[half:half + 1, :] = columns[half]
    pivoted = marks[:groups] + marks[groups:]

    rows_dev = reducers.shape[0]
    part = rows_dev // PANELS
    own = pivots[:, pl.ds(pl.multiple_of((owner // 2) * LANES, LANES), LANES)].astype(jnp.float32)
    row_ids = lax.broadcasted_iota(jnp.int32, (rows_dev, LANES), 0)
    lane_ids = lax.broadcasted_iota(jnp.int32, (rows_dev, LANES), 1)
    chosen = jnp.where(row_ids < part, own[0:1], own[1:2])
    target = (row_ids & (part - 1)) + part * core
    own_pivot = jnp.sum(jnp.where(lane_ids == target, chosen, 0.0), axis=1, keepdims=True)
    base = start.astype(jnp.float32)
    for group in range(groups):
        cols = slice(group * LANES, (group + 1) * LANES)
        here = (lane_ids + group * LANES).astype(jnp.float32) + base
        entries = centered(reducers[:, cols].astype(jnp.float32))
        pivot_value = jnp.where(here == own_pivot, 1.0, 0.0)
        normed[:, cols] = jnp.where(pivoted[group:group + 1] > 0.0, pivot_value, entries).astype(jnp.bfloat16)
    writes = [pltpu.make_async_copy(normed, copies.at[chip], done.at[chip]) for chip in range(copies.shape[0])]
    for write in writes:
        write.start()

    first = counts[owner - core]
    mine = counts[owner]
    values = rows[...].astype(jnp.float32).astype(jnp.bfloat16)
    slot_ids = lax.broadcasted_iota(jnp.int32, (capacity, capacity), 1)
    places = lax.broadcasted_iota(jnp.int32, (capacity, capacity), 0)
    places = (places + LIVE_DEV * core) & (capacity - 1)
    pick = one_hot((slot_ids < mine) & (slot_ids == places - core * first))
    values = dot(pick, values, NN).astype(jnp.bfloat16)
    placed[...] = values

    want = lax.broadcasted_iota(jnp.int32, (CAP, width), 0).astype(jnp.float32)
    here = jnp.where(core == 0, columns[0], columns[1])
    there = jnp.where(core == 0, columns[1], columns[0])
    keep[...] = centered(dot(one_hot(here == want), values, NT)).astype(jnp.int32).astype(jnp.int16)
    other = centered(dot(one_hot(there == want), values, NT)).astype(jnp.int32).astype(jnp.int16)
    send[:, :LIVE_DEV] = other[:, LIVE_DEV:]
    send[:, LIVE_DEV:] = other[:, :LIVE_DEV]
    for write in writes:
        write.wait()


def ranks_kernel(pivots, ranks, slots, most):
    core = lax.axis_index("core")
    count = pivots.shape[1]
    chunks = 32768 // LANES
    lane_rows = lax.broadcasted_iota(jnp.int32, (LANES, count), 0)
    chunk_rows = lax.broadcasted_iota(jnp.int32, (chunks, count), 0)
    side = (lax.broadcasted_iota(jnp.int32, (1, count), 1) >> 6) & 1
    chunk_marks, lane_marks = [], []
    marks = [jnp.zeros((chunks, LANES), jnp.float32)] * 2
    for panel in range(PANELS):
        pivot = pivots[panel:panel + 1, :]
        chunk = pivot >> 7
        chunk_marks.append(one_hot(chunk_rows == chunk))
        lane_marks.append(lane_rows == (pivot & (LANES - 1)))
        lane_hot = one_hot(lane_marks[-1])
        for half in range(2):
            marks[half] += dot(one_hot(chunk_rows == jnp.where(side == half, chunk, -1)), lane_hot, NT)
    here = lax.broadcasted_iota(jnp.int32, (chunks, chunks), 0)
    other = lax.broadcasted_iota(jnp.int32, (chunks, chunks), 1)
    block, other_block = here >> 3, other >> 3
    earlier = one_hot(((block == other_block) & (other < here)) | (block == other_block + 16))
    tables = []
    for half in range(2):
        flags = marks[half].astype(jnp.bfloat16)
        totals = dot(flags, jnp.ones((LANES, LANES), jnp.bfloat16), NN).astype(jnp.bfloat16)
        tables.append(dot(flags, strictly_before(LANES), NN) + dot(earlier, totals, NN))
    most[0] = jnp.max(jnp.maximum(
        jnp.where(marks[0] > 0.0, tables[0], 0.0), jnp.where(marks[1] > 0.0, tables[1], 0.0)
    )).astype(jnp.int32)
    table = jnp.where(core == 0, tables[0], tables[1])
    high = jnp.floor(table * (1.0 / 128.0))
    low = (table - 128.0 * high).astype(jnp.bfloat16)
    high = high.astype(jnp.bfloat16)
    grids = []
    for panel in range(PANELS):
        found = 128.0 * dot(high, chunk_marks[panel], TN) + dot(low, chunk_marks[panel], TN)
        rank = jnp.sum(jnp.where(lane_marks[panel], found, 0.0), axis=0, keepdims=True).astype(jnp.int32)
        slot = ((pivots[panel:panel + 1, :] >> 10) & 15) * CAP + rank
        for value in (rank, slot):
            grids.append(jnp.concatenate([value[:, i * LANES:(i + 1) * LANES] for i in range(count // LANES)], axis=0))
    left = lax.broadcasted_iota(jnp.int32, grids[0].shape, 1) < LANES // 2
    for out, a, b in ((ranks, grids[0], grids[2]), (slots, grids[1], grids[3])):
        firsts = jnp.where(left, a, pltpu.roll(b, LANES // 2, axis=1))
        seconds = jnp.where(left, pltpu.roll(a, LANES // 2, axis=1), b)
        out[...] = jnp.where(core == 0, firsts, seconds)


VMEM = pl.BlockSpec(memory_space=pltpu.VMEM)
SMEM = pl.BlockSpec(memory_space=pltpu.SMEM)


def front(counts, pivots, rows, reducers, chips):
    capacity, width = rows.shape
    packed = jax.ShapeDtypeStruct((CAP, capacity), jnp.int16)
    return pl.pallas_call(
        front_kernel,
        out_shape=(
            jax.ShapeDtypeStruct((chips, *reducers.shape), jnp.bfloat16),
            jax.ShapeDtypeStruct((capacity, width), jnp.bfloat16),
            packed,
            packed,
            jax.ShapeDtypeStruct((2, width), jnp.float32),
        ),
        in_specs=[SMEM, VMEM, VMEM, VMEM],
        out_specs=(pl.BlockSpec(memory_space=pl.ANY), VMEM, VMEM, VMEM, VMEM),
        scratch_shapes=[pltpu.VMEM(reducers.shape, jnp.bfloat16), pltpu.SemaphoreType.DMA((chips,))],
        name="front",
    )(counts, pivots, rows, reducers)


def ranks(pivots):
    grid = jax.ShapeDtypeStruct((pivots.shape[1] // LANES, LANES), jnp.int32)
    return pl.pallas_call(
        ranks_kernel,
        out_shape=(grid, grid, jax.ShapeDtypeStruct((1,), jnp.int32)),
        in_specs=[VMEM],
        out_specs=(VMEM, VMEM, SMEM),
        name="ranks",
        compiler_params=pltpu.CompilerParams(vmem_limit_bytes=16 << 20),
        cost_estimate=pl.CostEstimate(flops=2_000_000_000, bytes_accessed=1_000_000, transcendentals=0),
    )(pivots)


def shards(pair_rows, reducers, pivots, counts):
    core = lax.axis_index("core")
    chips = lax.axis_size(CHIP)
    col_width = pair_rows.shape[1]
    rows_dev = PANELS * reducers.shape[1]
    half = chips * rows_dev
    copies, placed, keep, send, columns = front(counts, pivots, pair_rows, reducers.reshape(rows_dev, col_width), chips)
    my_rank, my_slot, most = ranks(pivots)
    my_rank, my_slot = my_rank.reshape(-1), my_slot.reshape(-1)
    rounds = most[0] // CAP + 1

    def gather(keep, send, base):
        both = keep + swap(send, "core")
        both = both + swap(both, "yl")
        spread = lax.all_gather(both, "z", axis=0, tiled=True)
        here = jnp.where((my_rank >= base) & (my_rank < base + CAP), my_slot - base, -1)
        table = (here[:, None] == lax.iota(jnp.int32, spread.shape[0])[None, :]).astype(jnp.bfloat16)
        factors = dot(table, spread.astype(jnp.bfloat16), NN)
        return factors.astype(jnp.bfloat16)

    panel = lax.all_to_all(copies, CHIP, 0, 0, tiled=True).reshape(half, col_width)
    factors = gather(keep, send, 0)

    def another(state):
        step, factors = state
        base = step * CAP
        want = (lax.iota(jnp.int32, CAP) + base).astype(jnp.float32)
        more = [
            centered(dot((columns[side] == want[:, None]).astype(jnp.bfloat16), placed, NT)).astype(jnp.int16)
            for side in range(2)
        ]
        keep = jnp.where(core == 0, more[0], more[1])
        send = jnp.roll(jnp.where(core == 0, more[1], more[0]), LIVE_DEV, axis=1)
        return step + 1, factors + gather(keep, send, base)

    _, factors = lax.while_loop(lambda state: state[0] < rounds, another, (jnp.int32(1), factors))

    def reduced(start):
        rows = slice(start, start + LIVE_DEV)
        return remainder(placed[rows].astype(jnp.float32) - dot(factors[:, rows], panel, TN))

    incoming = swap(reduced(LIVE_DEV).astype(jnp.bfloat16), "core")
    own = lax.optimization_barrier(reduced(0))
    result = own + incoming.astype(jnp.float32)
    return jnp.where(result >= modulus, result - modulus, result).astype(jnp.int32)


def solution(mesh):
    fine = Mesh(mesh.devices.reshape(2, 4, 2, 2, 16), (*ROW, *COL))
    return jax.shard_map(
        shards,
        mesh=fine,
        in_specs=(P(ROW, COL), P(None, ROW, COL), P(), P()),
        out_specs=P(ROW, COL),
        check_vma=False,
    )
```

```python
import functools

import jax
import jax.numpy as jnp
from jax import lax
from jax.experimental import pallas as pl
from jax.experimental.pallas import tpu as pltpu
from jax.sharding import Mesh, PartitionSpec as P


PANELS = 2
LIVE_DEV = 256
CAP = 96
LANES = 128

ROW = ("yh", "x", "core")
COL = ("yl", "z")
CHIP = ("yh", "x")

modulus = 241.0
half_modulus = 120.0

NN = (((1,), (0,)), ((), ()))
NT = (((1,), (1,)), ((), ()))
TN = (((0,), (0,)), ((), ()))


def centered(values):
    return values - modulus * (values > half_modulus).astype(values.dtype)


def remainder(values):
    rest = values - modulus * jnp.floor(values * (1.0 / modulus))
    rest = jnp.where(rest < 0.0, rest + modulus, rest)
    return jnp.where(rest >= modulus, rest - modulus, rest)


def swap(value, axis):
    return lax.ppermute(value, axis, [(0, 1), (1, 0)])


def dot(left, right, dims):
    return lax.dot_general(left, right, dims, preferred_element_type=jnp.float32)


def spread_row(grid):
    return jnp.concatenate([grid[i:i + 1] for i in range(grid.shape[0])], axis=1)


def one_hot(hits):
    return hits.astype(jnp.float32).astype(jnp.bfloat16)


def strictly_before(size):
    lower = lax.broadcasted_iota(jnp.int32, (size, size), 0)
    upper = lax.broadcasted_iota(jnp.int32, (size, size), 1)
    return one_hot(lower < upper)


def front_kernel(
    counts, pivots, rows_in, reducers_in, copies, placed, keep, send, slots, rows, reducers, normed, done, come
):
    reads = [
        pltpu.make_async_copy(reducers_in, reducers, come.at[0]),
        pltpu.make_async_copy(rows_in, rows, come.at[1]),
    ]
    for read in reads:
        read.start()
    width = rows.shape[1]
    capacity = rows.shape[0]
    groups = width // LANES
    core = lax.axis_index("core")
    upper = lax.axis_index("yl")
    depth = lax.axis_index("z")
    owner = (lax.axis_index("yh") * 4 + lax.axis_index("x")) * 2 + core
    start = (upper * 16 + depth) * width

    count = pivots.shape[1]
    lane_rows = lax.broadcasted_iota(jnp.int32, (LANES, count), 0)
    group_rows = lax.broadcasted_iota(jnp.int32, (2 * groups, count), 0)
    side = (lax.broadcasted_iota(jnp.int32, (1, count), 1) >> 6) & 1
    marks = jnp.zeros((2 * groups, LANES), jnp.float32)
    ahead = [jnp.zeros((1, 1), jnp.float32)] * 2
    for panel in range(PANELS):
        pivot = pivots[panel:panel + 1, :]
        place = pivot - start
        high = jnp.where((place >= 0) & (place < width), (place >> 7) + side * groups, -1)
        marks += dot(one_hot(group_rows == high), one_hot(lane_rows == (place & (LANES - 1))), NT)
        for half in range(2):
            first_block = ((pivot >> 10) == depth) & (side == half)
            ahead[half] += jnp.sum(first_block.astype(jnp.float32), axis=1, keepdims=True)
    flags = marks.astype(jnp.bfloat16)
    inside = dot(flags, strictly_before(LANES), NN)
    totals = dot(flags, jnp.ones((LANES, LANES), jnp.bfloat16), NN)
    group_ids = lax.broadcasted_iota(jnp.int32, (groups, LANES), 0)
    columns = []
    for half in range(2):
        part = slice(half * groups, (half + 1) * groups)
        place = inside[part] + jnp.where(upper == 0, 0.0, ahead[half])
        for group in range(groups - 1):
            place += jnp.where(group_ids > group, totals[half * groups + group:half * groups + group + 1], 0.0)
        columns.append(spread_row(jnp.where(marks[part] > 0.0, place, -1.0)))
    pivoted = marks[:groups] + marks[groups:]

    rows_dev = reducers.shape[0]
    part = rows_dev // PANELS
    own = pivots[:, pl.ds(pl.multiple_of((owner // 2) * LANES, LANES), LANES)].astype(jnp.float32)
    row_ids = lax.broadcasted_iota(jnp.int32, (rows_dev, LANES), 0)
    lane_ids = lax.broadcasted_iota(jnp.int32, (rows_dev, LANES), 1)
    chosen = jnp.where(row_ids < part, own[0:1], own[1:2])
    target = (row_ids & (part - 1)) + part * core
    own_pivot = jnp.sum(jnp.where(lane_ids == target, chosen, 0.0), axis=1, keepdims=True)
    base = start.astype(jnp.float32)
    reads[0].wait()
    for group in range(groups):
        cols = slice(group * LANES, (group + 1) * LANES)
        here = (lane_ids + group * LANES).astype(jnp.float32) + base
        entries = centered(reducers[:, cols].astype(jnp.float32))
        pivot_value = jnp.where(here == own_pivot, 1.0, 0.0)
        normed[:, cols] = jnp.where(pivoted[group:group + 1] > 0.0, pivot_value, entries).astype(jnp.bfloat16)
    writes = [pltpu.make_async_copy(normed, copies.at[chip], done.at[chip]) for chip in range(copies.shape[0])]
    for write in writes:
        write.start()

    first = counts[owner - core]
    mine = counts[owner]
    slot_ids = lax.broadcasted_iota(jnp.int32, (capacity, capacity), 1)
    places = lax.broadcasted_iota(jnp.int32, (capacity, capacity), 0)
    places = (places + LIVE_DEV * core) & (capacity - 1)
    pick = one_hot((slot_ids < mine) & (slot_ids == places - core * first))
    reads[1].wait()
    values = rows[...].astype(jnp.float32).astype(jnp.bfloat16)
    values = dot(pick, values, NN).astype(jnp.bfloat16)
    placed[...] = values

    want = lax.broadcasted_iota(jnp.int32, (CAP, width), 0).astype(jnp.float32)
    here = jnp.where(core == 0, columns[0], columns[1])
    there = jnp.where(core == 0, columns[1], columns[0])
    slots[0:1, :], slots[1:2, :] = here, there
    keep[...] = centered(dot(one_hot(here == want), values, NT)).astype(jnp.int32).astype(jnp.int16)
    other = centered(dot(one_hot(there == want), values, NT)).astype(jnp.int32).astype(jnp.int16)
    send[:, :LIVE_DEV] = other[:, LIVE_DEV:]
    send[:, LIVE_DEV:] = other[:, :LIVE_DEV]
    for write in writes:
        write.wait()


def ranks_kernel(pivots, ranks, slots, firsts, extra):
    core = lax.axis_index("core")
    count = pivots.shape[1]
    chunks = 32768 // LANES
    both = 2 * LANES
    lane_rows = lax.broadcasted_iota(jnp.int32, (both, count), 0)
    chunk_rows = lax.broadcasted_iota(jnp.int32, (chunks, count), 0)
    side = (lax.broadcasted_iota(jnp.int32, (1, count), 1) >> 6) & 1
    chunk_marks = []
    marks = jnp.zeros((chunks, both), jnp.float32)
    for panel in range(PANELS):
        pivot = pivots[panel:panel + 1, :]
        chunk_marks.append(one_hot(chunk_rows == (pivot >> 7)))
        marks += dot(chunk_marks[-1], one_hot(lane_rows == ((pivot & (LANES - 1)) + side * LANES)), NT)
    flags = marks.astype(jnp.bfloat16)
    here = lax.broadcasted_iota(jnp.int32, (chunks, chunks), 0)
    other = lax.broadcasted_iota(jnp.int32, (chunks, chunks), 1)
    block, other_block = here >> 3, other >> 3
    earlier = one_hot(((block == other_block) & (other < here)) | (block == other_block + 16))
    same_side = (here >> 7) == (other >> 7)
    totals = dot(flags, one_hot(same_side), NN).astype(jnp.bfloat16)
    table = dot(flags, one_hot(same_side & (here < other)), NN) + dot(earlier, totals, NN)
    extra[0] = jnp.max(jnp.where(marks > 0.0, table, 0.0)).astype(jnp.int32) // CAP
    table = jnp.where(core == 0, table[:, :LANES], table[:, LANES:])
    high = jnp.floor(table * (1.0 / 128.0))
    parts = jnp.concatenate([high, table - 128.0 * high], axis=1).astype(jnp.bfloat16)
    grids = []
    for panel in range(PANELS):
        pivot = pivots[panel:panel + 1, :]
        found = dot(parts, chunk_marks[panel], TN)
        found = 128.0 * found[:LANES] + found[LANES:]
        rank = jnp.where(lane_rows[:LANES] == (pivot & (LANES - 1)), found, 0.0)
        rank = jnp.sum(rank, axis=0, keepdims=True).astype(jnp.int32)
        for value in (rank, ((pivot >> 10) & 15) * CAP + rank):
            grids.append(jnp.concatenate([value[:, i * LANES:(i + 1) * LANES] for i in range(count // LANES)], axis=0))
    left = lax.broadcasted_iota(jnp.int32, grids[0].shape, 1) < LANES // 2
    picked = []
    for a, b in ((grids[0], grids[2]), (grids[1], grids[3])):
        lows = jnp.where(left, a, pltpu.roll(b, LANES // 2, axis=1))
        highs = jnp.where(left, pltpu.roll(a, LANES // 2, axis=1), b)
        picked.append(jnp.where(core == 0, lows, highs))
    ranks[...], slots[...] = picked
    firsts[...] = jnp.where(picked[0] < CAP, picked[1], -1)


def reduce_kernel(first_row, spread, where, placed, panel_in, out, panel, come):
    depth = 2 * LANES
    blocks = panel.shape[0] // depth
    reads = []
    for block in range(blocks):
        part = pl.ds(block * depth, depth)
        reads.append(pltpu.make_async_copy(panel_in.at[part], panel.at[part], come.at[block]))
        reads[block].start()
    rows = slice(first_row, first_row + LIVE_DEV)
    slot_count = spread.shape[0]
    packed = jnp.transpose(spread[:, rows].astype(jnp.int32).astype(jnp.float32)).astype(jnp.bfloat16)
    slot_rows = lax.broadcasted_iota(jnp.int32, (slot_count, depth), 0)
    total = jnp.zeros(out.shape, jnp.float32)
    for block in range(blocks):
        here = spread_row(where[2 * block:2 * block + 2, :])
        factors = dot(packed, one_hot(slot_rows == here), NN).astype(jnp.bfloat16)
        reads[block].wait()
        total += dot(factors, panel[block * depth:(block + 1) * depth, :], NN)
    out[...] = remainder(placed[rows, :].astype(jnp.float32) - total).astype(jnp.bfloat16)


def combine_kernel(own, incoming, out, result, done):
    step = LIVE_DEV // done.shape[0]
    writes = []
    for part in range(done.shape[0]):
        rows = slice(part * step, (part + 1) * step)
        total = own[rows, :].astype(jnp.float32) + incoming[rows, :].astype(jnp.float32)
        result[rows, :] = jnp.where(total >= modulus, total - modulus, total).astype(jnp.int32)
        write = pltpu.make_async_copy(result.at[pl.ds(part * step, step)], out.at[pl.ds(part * step, step)], done.at[part])
        write.start()
        writes.append(write)
    for write in writes:
        write.wait()


VMEM = pl.BlockSpec(memory_space=pltpu.VMEM)
SMEM = pl.BlockSpec(memory_space=pltpu.SMEM)
ANY = pl.BlockSpec(memory_space=pl.ANY)


def front(counts, pivots, rows, reducers, chips):
    capacity, width = rows.shape
    packed = jax.ShapeDtypeStruct((CAP, capacity), jnp.int16)
    return pl.pallas_call(
        front_kernel,
        out_shape=(
            jax.ShapeDtypeStruct((chips, *reducers.shape), jnp.bfloat16),
            jax.ShapeDtypeStruct((capacity, width), jnp.bfloat16),
            packed,
            packed,
            jax.ShapeDtypeStruct((2, width), jnp.float32),
        ),
        in_specs=[SMEM, VMEM, ANY, ANY],
        out_specs=(ANY, VMEM, VMEM, VMEM, VMEM),
        scratch_shapes=[
            pltpu.VMEM(rows.shape, jnp.int32),
            pltpu.VMEM(reducers.shape, jnp.int32),
            pltpu.VMEM(reducers.shape, jnp.bfloat16),
            pltpu.SemaphoreType.DMA((chips,)),
            pltpu.SemaphoreType.DMA((2,)),
        ],
        name="front",
    )(counts, pivots, rows, reducers)


def ranks(pivots):
    grid = jax.ShapeDtypeStruct((pivots.shape[1] // LANES, LANES), jnp.int32)
    return pl.pallas_call(
        ranks_kernel,
        out_shape=(grid, grid, grid, jax.ShapeDtypeStruct((1,), jnp.int32)),
        in_specs=[VMEM],
        out_specs=(VMEM, VMEM, VMEM, SMEM),
        name="ranks",
        compiler_params=pltpu.CompilerParams(vmem_limit_bytes=16 << 20),
        cost_estimate=pl.CostEstimate(flops=2_000_000_000, bytes_accessed=1_000_000, transcendentals=0),
    )(pivots)


def reduced(first_row, spread, where, placed, panel):
    width = panel.shape[1]
    return pl.pallas_call(
        functools.partial(reduce_kernel, first_row),
        out_shape=jax.ShapeDtypeStruct((LIVE_DEV, width), jnp.bfloat16),
        in_specs=[VMEM, VMEM, VMEM, ANY],
        out_specs=VMEM,
        scratch_shapes=[pltpu.VMEM(panel.shape, jnp.bfloat16), pltpu.SemaphoreType.DMA((panel.shape[0] // (2 * LANES),))],
        compiler_params=pltpu.CompilerParams(vmem_limit_bytes=24 << 20),
        cost_estimate=pl.CostEstimate(flops=1_500_000_000, bytes_accessed=5_000_000, transcendentals=0),
    )(spread, where, placed, panel)


def combine(own, incoming):
    return pl.pallas_call(
        combine_kernel,
        out_shape=jax.ShapeDtypeStruct(own.shape, jnp.int32),
        in_specs=[VMEM] * 2,
        out_specs=pl.BlockSpec(memory_space=pltpu.HBM),
        scratch_shapes=[pltpu.VMEM(own.shape, jnp.int32), pltpu.SemaphoreType.DMA((4,))],
        name="combine",
        compiler_params=pltpu.CompilerParams(vmem_limit_bytes=8 << 20),
    )(own, incoming)


def shards(pair_rows, reducers, pivots, counts):
    chips = lax.axis_size(CHIP)
    col_width = pair_rows.shape[1]
    rows_dev = PANELS * reducers.shape[1]
    half = chips * rows_dev
    copies, placed, keep, send, columns = front(counts, pivots, pair_rows, reducers.reshape(rows_dev, col_width), chips)
    my_rank, my_slot, firsts, extra = ranks(pivots)

    def gather(keep, send):
        both = keep + swap(send, "core")
        both = both + swap(both, "yl")
        return lax.all_gather(both, "z", axis=0, tiled=True)

    panel = lax.all_to_all(copies, CHIP, 0, 0, tiled=True).reshape(half, col_width)
    spread = gather(keep, send)
    incoming = reduced(LIVE_DEV, spread, firsts, placed, panel)
    incoming = swap(incoming, "core")
    own = reduced(0, spread, firsts, placed, panel)
    first = combine(own, incoming)

    def another(state):
        step, result = state
        base = step * CAP
        want = (lax.iota(jnp.int32, CAP) + base).astype(jnp.float32)
        keep, send = [
            centered(dot((columns[side] == want[:, None]).astype(jnp.bfloat16), placed, NT)).astype(jnp.int16)
            for side in range(2)
        ]
        spread = gather(keep, jnp.roll(send, LIVE_DEV, axis=1)).astype(jnp.bfloat16)
        where = jnp.where((my_rank >= base) & (my_rank < base + CAP), my_slot - base, -1).reshape(-1, 1)
        table = (where == lax.iota(jnp.int32, spread.shape[0])[None, :]).astype(jnp.bfloat16)
        products = remainder(dot(dot(table, spread, NN).astype(jnp.bfloat16), panel, TN))
        incoming = swap(products[LIVE_DEV:].astype(jnp.bfloat16), "core").astype(jnp.float32)
        result = result.astype(jnp.float32) - products[:LIVE_DEV] - incoming
        return step - 1, remainder(result).astype(jnp.int32)

    _, result = lax.while_loop(lambda state: state[0] > 0, another, (extra[0], first))
    return result


def solution(mesh):
    fine = Mesh(mesh.devices.reshape(2, 4, 2, 2, 16), (*ROW, *COL))
    return jax.shard_map(
        shards,
        mesh=fine,
        in_specs=(P(ROW, COL), P(None, ROW, COL), P(), P()),
        out_specs=P(ROW, COL),
        check_vma=False,
    )
```

```python
import functools

import jax
import jax.numpy as jnp
from jax import lax
from jax.experimental import pallas as pl
from jax.experimental.pallas import tpu as pltpu
from jax.sharding import Mesh, PartitionSpec as P


PANELS = 2
LIVE_DEV = 256
CAP = 96
LANES = 128

ROW = ("yh", "x", "core")
COL = ("yl", "z")
CHIP = ("yh", "x")

modulus = 241.0
half_modulus = 120.0

NN = (((1,), (0,)), ((), ()))
NT = (((1,), (1,)), ((), ()))
TN = (((0,), (0,)), ((), ()))


def centered(values):
    return values - modulus * (values > half_modulus).astype(values.dtype)


def remainder(values):
    rest = values - modulus * jnp.floor(values * (1.0 / modulus))
    rest = jnp.where(rest < 0.0, rest + modulus, rest)
    return jnp.where(rest >= modulus, rest - modulus, rest)


def swap(value, axis):
    return lax.ppermute(value, axis, [(0, 1), (1, 0)])


def dot(left, right, dims):
    return lax.dot_general(left, right, dims, preferred_element_type=jnp.float32)


def spread_row(grid):
    return jnp.concatenate([grid[i:i + 1] for i in range(grid.shape[0])], axis=1)


def one_hot(hits):
    return hits.astype(jnp.float32).astype(jnp.bfloat16)


def strictly_before(size):
    lower = lax.broadcasted_iota(jnp.int32, (size, size), 0)
    upper = lax.broadcasted_iota(jnp.int32, (size, size), 1)
    return one_hot(lower < upper)


def front_kernel(counts, pivots, rows, reducers, copies, placed, keep, send, slots, normed, done):
    width = rows.shape[1]
    capacity = rows.shape[0]
    groups = width // LANES
    core = lax.axis_index("core")
    upper = lax.axis_index("yl")
    depth = lax.axis_index("z")
    owner = (lax.axis_index("yh") * 4 + lax.axis_index("x")) * 2 + core
    start = (upper * 16 + depth) * width

    count = pivots.shape[1]
    lane_rows = lax.broadcasted_iota(jnp.int32, (LANES, count), 0)
    group_rows = lax.broadcasted_iota(jnp.int32, (2 * groups, count), 0)
    side = (lax.broadcasted_iota(jnp.int32, (1, count), 1) >> 6) & 1
    marks = jnp.zeros((2 * groups, LANES), jnp.float32)
    ahead = [jnp.zeros((1, 1), jnp.float32)] * 2
    for panel in range(PANELS):
        pivot = pivots[panel:panel + 1, :]
        place = pivot - start
        high = jnp.where((place >= 0) & (place < width), (place >> 7) + side * groups, -1)
        marks += dot(one_hot(group_rows == high), one_hot(lane_rows == (place & (LANES - 1))), NT)
        for half in range(2):
            first_block = ((pivot >> 10) == depth) & (side == half)
            ahead[half] += jnp.sum(first_block.astype(jnp.float32), axis=1, keepdims=True)
    flags = marks.astype(jnp.bfloat16)
    inside = dot(flags, strictly_before(LANES), NN)
    totals = dot(flags, jnp.ones((LANES, LANES), jnp.bfloat16), NN)
    group_ids = lax.broadcasted_iota(jnp.int32, (groups, LANES), 0)
    columns = []
    for half in range(2):
        part = slice(half * groups, (half + 1) * groups)
        place = inside[part] + jnp.where(upper == 0, 0.0, ahead[half])
        for group in range(groups - 1):
            place += jnp.where(group_ids > group, totals[half * groups + group:half * groups + group + 1], 0.0)
        columns.append(spread_row(jnp.where(marks[part] > 0.0, place, -1.0)))
    pivoted = marks[:groups] + marks[groups:]

    rows_dev = reducers.shape[0]
    part = rows_dev // PANELS
    own = pivots[:, pl.ds(pl.multiple_of((owner // 2) * LANES, LANES), LANES)].astype(jnp.float32)
    row_ids = lax.broadcasted_iota(jnp.int32, (rows_dev, LANES), 0)
    lane_ids = lax.broadcasted_iota(jnp.int32, (rows_dev, LANES), 1)
    chosen = jnp.where(row_ids < part, own[0:1], own[1:2])
    target = (row_ids & (part - 1)) + part * core
    own_pivot = jnp.sum(jnp.where(lane_ids == target, chosen, 0.0), axis=1, keepdims=True)
    base = start.astype(jnp.float32)
    for group in range(groups):
        cols = slice(group * LANES, (group + 1) * LANES)
        here = (lane_ids + group * LANES).astype(jnp.float32) + base
        entries = centered(reducers[:, cols].astype(jnp.float32))
        pivot_value = jnp.where(here == own_pivot, 1.0, 0.0)
        normed[:, cols] = jnp.where(pivoted[group:group + 1] > 0.0, pivot_value, entries).astype(jnp.bfloat16)
    writes = [pltpu.make_async_copy(normed, copies.at[chip], done.at[chip]) for chip in range(copies.shape[0])]
    for write in writes:
        write.start()

    first = counts[owner - core]
    mine = counts[owner]
    slot_ids = lax.broadcasted_iota(jnp.int32, (capacity, capacity), 1)
    places = lax.broadcasted_iota(jnp.int32, (capacity, capacity), 0)
    places = (places + LIVE_DEV * core) & (capacity - 1)
    pick = one_hot((slot_ids < mine) & (slot_ids == places - core * first))
    values = rows[...].astype(jnp.float32).astype(jnp.bfloat16)
    values = dot(pick, values, NN).astype(jnp.bfloat16)
    placed[...] = values

    want = lax.broadcasted_iota(jnp.int32, (CAP, width), 0).astype(jnp.float32)
    here = jnp.where(core == 0, columns[0], columns[1])
    there = jnp.where(core == 0, columns[1], columns[0])
    slots[0:1, :], slots[1:2, :] = here, there
    choose = jnp.concatenate([one_hot(here == want), one_hot(there == want)], axis=0)
    packed = centered(dot(choose, values, NT)).astype(jnp.int32).astype(jnp.int16)
    keep[...] = packed[:CAP]
    other = packed[CAP:]
    send[:, :LIVE_DEV] = other[:, LIVE_DEV:]
    send[:, LIVE_DEV:] = other[:, :LIVE_DEV]
    for write in writes:
        write.wait()


def ranks_kernel(pivots, ranks, slots, firsts, extra):
    core = lax.axis_index("core")
    count = pivots.shape[1]
    chunks = 32768 // LANES
    pieces = count // LANES

    pair_rows = lax.broadcasted_iota(jnp.int32, (32, count), 0)
    side = (lax.broadcasted_iota(jnp.int32, (1, count), 1) >> 6) & 1
    counted = jnp.zeros((32, 1), jnp.float32)
    grids = []
    for panel in range(PANELS):
        pivot = pivots[panel:panel + 1, :]
        hits = (pair_rows == ((pivot >> 10) & 15) + 16 * side).astype(jnp.float32)
        counted += jnp.sum(hits, axis=1, keepdims=True)
        grids.append(jnp.concatenate([pivot[:, i * LANES:(i + 1) * LANES] for i in range(pieces)], axis=0))
    extra[0] = (jnp.max(counted).astype(jnp.int32) - 1) // CAP

    left = lax.broadcasted_iota(jnp.int32, grids[0].shape, 1) < LANES // 2
    lows = jnp.where(left, grids[0], pltpu.roll(grids[1], LANES // 2, axis=1))
    highs = jnp.where(left, pltpu.roll(grids[0], LANES // 2, axis=1), grids[1])
    own = jnp.where(core == 0, lows, highs)
    pivot = spread_row(own)
    chunk_hot = one_hot(lax.broadcasted_iota(jnp.int32, (chunks, count), 0) == (pivot >> 7))
    lane_hits = lax.broadcasted_iota(jnp.int32, (LANES, count), 0) == (pivot & (LANES - 1))
    flags = dot(chunk_hot, one_hot(lane_hits), NT).astype(jnp.bfloat16)
    here = lax.broadcasted_iota(jnp.int32, (chunks, chunks), 0)
    other = lax.broadcasted_iota(jnp.int32, (chunks, chunks), 1)
    block, other_block = here >> 3, other >> 3
    earlier = one_hot(((block == other_block) & (other < here)) | (block == other_block + 16))
    totals = dot(flags, jnp.ones((LANES, LANES), jnp.bfloat16), NN).astype(jnp.bfloat16)
    table = dot(flags, strictly_before(LANES), NN) + dot(earlier, totals, NN)
    high = jnp.floor(table * (1.0 / 128.0))
    parts = jnp.concatenate([high, table - 128.0 * high], axis=1).astype(jnp.bfloat16)
    found = dot(parts, chunk_hot, TN)
    found = 128.0 * found[:LANES] + found[LANES:]
    rank = jnp.sum(jnp.where(lane_hits, found, 0.0), axis=0, keepdims=True).astype(jnp.int32)
    rank = jnp.concatenate([rank[:, i * LANES:(i + 1) * LANES] for i in range(pieces)], axis=0)
    slot = ((own >> 10) & 15) * CAP + rank
    ranks[...] = rank
    slots[...] = slot
    firsts[...] = jnp.where(rank < CAP, slot, -1)


def unpack_kernel(spread, where, factors):
    slot_count = spread.shape[0]
    packed = spread[...].astype(jnp.int32).astype(jnp.float32).astype(jnp.bfloat16)
    slot_lanes = lax.broadcasted_iota(jnp.int32, (2 * LANES, slot_count), 1)
    square = (LANES, LANES)
    diagonal = lax.broadcasted_iota(jnp.int32, square, 0) == lax.broadcasted_iota(jnp.int32, square, 1)
    for block in range(where.shape[0] // 2):
        columns = [
            jnp.sum(
                jnp.where(diagonal, where[piece:piece + 1, :].astype(jnp.float32), 0.0), axis=1, keepdims=True
            )
            for piece in (2 * block, 2 * block + 1)
        ]
        here = jnp.concatenate(columns, axis=0).astype(jnp.int32)
        rows = slice(block * 2 * LANES, (block + 1) * 2 * LANES)
        factors[rows, :] = dot(one_hot(slot_lanes == here), packed, NN).astype(jnp.bfloat16)


def reduce_kernel(first_row, factors, placed, panel, out, values, come):
    read = pltpu.make_async_copy(placed.at[pl.ds(first_row, LIVE_DEV)], values, come)
    read.start()
    turned = jnp.transpose(factors[:, first_row:first_row + LIVE_DEV])
    step = panel.shape[1] // 4
    for part in range(4):
        cols = slice(part * step, (part + 1) * step)
        product = dot(turned, panel[:, cols], NN)
        if part == 0:
            read.wait()
        out[:, cols] = remainder(values[:, cols].astype(jnp.float32) - product).astype(jnp.bfloat16)


def combine_kernel(own, incoming, out, result, done):
    step = LIVE_DEV // done.shape[0]
    writes = []
    for part in range(done.shape[0]):
        rows = slice(part * step, (part + 1) * step)
        total = own[rows, :].astype(jnp.float32) + incoming[rows, :].astype(jnp.float32)
        result[rows, :] = jnp.where(total >= modulus, total - modulus, total).astype(jnp.int32)
        write = pltpu.make_async_copy(result.at[pl.ds(part * step, step)], out.at[pl.ds(part * step, step)], done.at[part])
        write.start()
        writes.append(write)
    for write in writes:
        write.wait()


VMEM = pl.BlockSpec(memory_space=pltpu.VMEM)
SMEM = pl.BlockSpec(memory_space=pltpu.SMEM)
ANY = pl.BlockSpec(memory_space=pl.ANY)


def front(counts, pivots, rows, reducers, chips):
    capacity, width = rows.shape
    packed = jax.ShapeDtypeStruct((CAP, capacity), jnp.int16)
    return pl.pallas_call(
        front_kernel,
        out_shape=(
            jax.ShapeDtypeStruct((chips, *reducers.shape), jnp.bfloat16),
            jax.ShapeDtypeStruct((capacity, width), jnp.bfloat16),
            packed,
            packed,
            jax.ShapeDtypeStruct((2, width), jnp.float32),
        ),
        in_specs=[SMEM, VMEM, VMEM, VMEM],
        out_specs=(ANY, VMEM, VMEM, VMEM, VMEM),
        scratch_shapes=[
            pltpu.VMEM(reducers.shape, jnp.bfloat16),
            pltpu.SemaphoreType.DMA((chips,)),
        ],
        name="front",
    )(counts, pivots, rows, reducers)


def ranks(pivots):
    grid = jax.ShapeDtypeStruct((pivots.shape[1] // LANES, LANES), jnp.int32)
    return pl.pallas_call(
        ranks_kernel,
        out_shape=(grid, grid, grid, jax.ShapeDtypeStruct((1,), jnp.int32)),
        in_specs=[VMEM],
        out_specs=(VMEM, VMEM, VMEM, SMEM),
        name="ranks",
        compiler_params=pltpu.CompilerParams(vmem_limit_bytes=16 << 20),
        cost_estimate=pl.CostEstimate(flops=2_000_000_000, bytes_accessed=1_000_000, transcendentals=0),
    )(pivots)


def unpacked(spread, where):
    return pl.pallas_call(
        unpack_kernel,
        out_shape=jax.ShapeDtypeStruct((where.shape[0] * LANES, spread.shape[1]), jnp.bfloat16),
        in_specs=[VMEM] * 2,
        out_specs=VMEM,
        name="unpack",
        compiler_params=pltpu.CompilerParams(vmem_limit_bytes=24 << 20),
        cost_estimate=pl.CostEstimate(flops=1_600_000_000, bytes_accessed=3_000_000, transcendentals=0),
    )(spread, where)


def reduced(first_row, factors, placed, panel):
    width = panel.shape[1]
    return pl.pallas_call(
        functools.partial(reduce_kernel, first_row),
        out_shape=jax.ShapeDtypeStruct((LIVE_DEV, width), jnp.bfloat16),
        in_specs=[VMEM, ANY, VMEM],
        out_specs=VMEM,
        scratch_shapes=[pltpu.VMEM((LIVE_DEV, width), jnp.bfloat16), pltpu.SemaphoreType.DMA],
        compiler_params=pltpu.CompilerParams(vmem_limit_bytes=24 << 20),
        cost_estimate=pl.CostEstimate(flops=540_000_000, bytes_accessed=4_000_000, transcendentals=0),
    )(factors, placed, panel)


def combine(own, incoming):
    return pl.pallas_call(
        combine_kernel,
        out_shape=jax.ShapeDtypeStruct(own.shape, jnp.int32),
        in_specs=[VMEM] * 2,
        out_specs=pl.BlockSpec(memory_space=pltpu.HBM),
        scratch_shapes=[pltpu.VMEM(own.shape, jnp.int32), pltpu.SemaphoreType.DMA((4,))],
        name="combine",
        compiler_params=pltpu.CompilerParams(vmem_limit_bytes=8 << 20),
    )(own, incoming)


def shards(pair_rows, reducers, pivots, counts):
    chips = lax.axis_size(CHIP)
    col_width = pair_rows.shape[1]
    rows_dev = PANELS * reducers.shape[1]
    half = chips * rows_dev
    blocks = (counts, pivots, pair_rows, reducers.reshape(rows_dev, col_width))
    copies, placed, keep, send, columns = front(*blocks, chips)
    my_rank, my_slot, firsts, extra = ranks(pivots)

    def gather(keep, send):
        both = keep + swap(send, "core")
        both = both + swap(both, "yl")
        return lax.all_gather(both, "z", axis=0, tiled=True)

    def fetch_panel(copies):
        return lax.all_to_all(copies, CHIP, 0, 0, tiled=True).reshape(half, col_width)

    def unpack(spread, where):
        table = (where.reshape(-1, 1) == lax.iota(jnp.int32, spread.shape[0])[None, :]).astype(jnp.bfloat16)
        return dot(table, spread.astype(jnp.bfloat16), NN).astype(jnp.bfloat16)

    panel = fetch_panel(copies)
    spread = gather(keep, send)

    factors = unpacked(spread, firsts)
    incoming = swap(reduced(LIVE_DEV, factors, placed, panel), "core")
    own = reduced(0, factors, placed, panel)
    first = combine(own, incoming)

    def another(state):
        step, result = state
        base = step * CAP
        want = (lax.iota(jnp.int32, CAP) + base).astype(jnp.float32)
        keep, send = [
            centered(dot((columns[side] == want[:, None]).astype(jnp.bfloat16), placed, NT)).astype(jnp.int16)
            for side in range(2)
        ]
        where = jnp.where((my_rank >= base) & (my_rank < base + CAP), my_slot - base, -1)
        factors = unpack(gather(keep, jnp.roll(send, LIVE_DEV, axis=1)), where)
        again, _ = lax.optimization_barrier((copies, step))
        products = remainder(dot(factors, fetch_panel(again), TN))
        incoming = swap(products[LIVE_DEV:].astype(jnp.bfloat16), "core").astype(jnp.float32)
        result = result.astype(jnp.float32) - products[:LIVE_DEV] - incoming
        return step - 1, remainder(result).astype(jnp.int32)

    _, result = lax.while_loop(lambda state: state[0] > 0, another, (extra[0], first))
    return result


def solution(mesh):
    fine = Mesh(mesh.devices.reshape(2, 4, 2, 2, 16), (*ROW, *COL))
    return jax.shard_map(
        shards,
        mesh=fine,
        in_specs=(P(ROW, COL), P(None, ROW, COL), P(), P()),
        out_specs=P(ROW, COL),
        check_vma=False,
    )
```

```python
import functools

import jax
import jax.numpy as jnp
from jax import lax
from jax.experimental import pallas as pl
from jax.experimental.pallas import tpu as pltpu
from jax.sharding import Mesh, PartitionSpec as P


PANELS = 2
LIVE_DEV = 256
CAP = 96
LANES = 128

ROW = ("yh", "x", "core")
COL = ("yl", "z")
CHIP = ("yh", "x")

modulus = 241.0
half_modulus = 120.0

NN = (((1,), (0,)), ((), ()))
NT = (((1,), (1,)), ((), ()))
TN = (((0,), (0,)), ((), ()))


def centered(values):
    return values - modulus * (values > half_modulus).astype(values.dtype)


def remainder(values):
    rest = values - modulus * jnp.floor(values * (1.0 / modulus))
    rest = jnp.where(rest < 0.0, rest + modulus, rest)
    return jnp.where(rest >= modulus, rest - modulus, rest)


def swap(value, axis):
    return lax.ppermute(value, axis, [(0, 1), (1, 0)])


def dot(left, right, dims):
    return lax.dot_general(left, right, dims, preferred_element_type=jnp.float32)


def spread_row(grid):
    return jnp.concatenate([grid[i:i + 1] for i in range(grid.shape[0])], axis=1)


def one_hot(hits):
    return hits.astype(jnp.float32).astype(jnp.bfloat16)


def strictly_before(size):
    lower = lax.broadcasted_iota(jnp.int32, (size, size), 0)
    upper = lax.broadcasted_iota(jnp.int32, (size, size), 1)
    return one_hot(lower < upper)


def front_kernel(counts, pivots, rows, reducers, copies, placed, keep, send, slots, normed, done):
    width = rows.shape[1]
    capacity = rows.shape[0]
    groups = width // LANES
    core = lax.axis_index("core")
    upper = lax.axis_index("yl")
    depth = lax.axis_index("z")
    owner = (lax.axis_index("yh") * 4 + lax.axis_index("x")) * 2 + core
    start = (upper * 16 + depth) * width

    count = pivots.shape[1]
    lane_rows = lax.broadcasted_iota(jnp.int32, (LANES, count), 0)
    group_rows = lax.broadcasted_iota(jnp.int32, (2 * groups, count), 0)
    side = (lax.broadcasted_iota(jnp.int32, (1, count), 1) >> 6) & 1
    marks = jnp.zeros((2 * groups, LANES), jnp.float32)
    ahead = [jnp.zeros((1, 1), jnp.float32)] * 2
    for panel in range(PANELS):
        pivot = pivots[panel:panel + 1, :]
        place = pivot - start
        high = jnp.where((place >= 0) & (place < width), (place >> 7) + side * groups, -1)
        marks += dot(one_hot(group_rows == high), one_hot(lane_rows == (place & (LANES - 1))), NT)
        for half in range(2):
            first_block = ((pivot >> 10) == depth) & (side == half)
            ahead[half] += jnp.sum(first_block.astype(jnp.float32), axis=1, keepdims=True)
    flags = marks.astype(jnp.bfloat16)
    inside = dot(flags, strictly_before(LANES), NN)
    totals = dot(flags, jnp.ones((LANES, LANES), jnp.bfloat16), NN)
    group_ids = lax.broadcasted_iota(jnp.int32, (groups, LANES), 0)
    columns = []
    for half in range(2):
        part = slice(half * groups, (half + 1) * groups)
        place = inside[part] + jnp.where(upper == 0, 0.0, ahead[half])
        for group in range(groups - 1):
            place += jnp.where(group_ids > group, totals[half * groups + group:half * groups + group + 1], 0.0)
        columns.append(spread_row(jnp.where(marks[part] > 0.0, place, -1.0)))
    pivoted = marks[:groups] + marks[groups:]

    rows_dev = reducers.shape[0]
    part = rows_dev // PANELS
    own = pivots[:, pl.ds(pl.multiple_of((owner // 2) * LANES, LANES), LANES)].astype(jnp.float32)
    row_ids = lax.broadcasted_iota(jnp.int32, (rows_dev, LANES), 0)
    lane_ids = lax.broadcasted_iota(jnp.int32, (rows_dev, LANES), 1)
    chosen = jnp.where(row_ids < part, own[0:1], own[1:2])
    target = (row_ids & (part - 1)) + part * core
    own_pivot = jnp.sum(jnp.where(lane_ids == target, chosen, 0.0), axis=1, keepdims=True)
    base = start.astype(jnp.float32)
    for group in range(groups):
        cols = slice(group * LANES, (group + 1) * LANES)
        here = (lane_ids + group * LANES).astype(jnp.float32) + base
        entries = centered(reducers[:, cols].astype(jnp.float32))
        pivot_value = jnp.where(here == own_pivot, 1.0, 0.0)
        normed[:, cols] = jnp.where(pivoted[group:group + 1] > 0.0, pivot_value, entries).astype(jnp.bfloat16)
    writes = [pltpu.make_async_copy(normed, copies.at[chip], done.at[chip]) for chip in range(copies.shape[0])]
    for write in writes:
        write.start()

    first = counts[owner - core]
    mine = counts[owner]
    slot_ids = lax.broadcasted_iota(jnp.int32, (capacity, capacity), 1)
    places = lax.broadcasted_iota(jnp.int32, (capacity, capacity), 0)
    places = (places + LIVE_DEV * core) & (capacity - 1)
    pick = one_hot((slot_ids < mine) & (slot_ids == places - core * first))
    values = rows[...].astype(jnp.float32).astype(jnp.bfloat16)
    values = dot(pick, values, NN).astype(jnp.bfloat16)
    placed[...] = values

    want = lax.broadcasted_iota(jnp.int32, (CAP, width), 0).astype(jnp.float32)
    here = jnp.where(core == 0, columns[0], columns[1])
    there = jnp.where(core == 0, columns[1], columns[0])
    slots[0:1, :], slots[1:2, :] = here, there
    choose = jnp.concatenate([one_hot(here == want), one_hot(there == want)], axis=0)
    packed = centered(dot(choose, values, NT)).astype(jnp.int32).astype(jnp.int16)
    keep[...] = packed[:CAP]
    other = packed[CAP:]
    send[:, :LIVE_DEV] = other[:, LIVE_DEV:]
    send[:, LIVE_DEV:] = other[:, :LIVE_DEV]
    for write in writes:
        write.wait()


def ranks_kernel(pivots, ranks, slots, firsts, extra):
    core = lax.axis_index("core")
    count = pivots.shape[1]
    chunks = 32768 // LANES
    pieces = count // LANES

    pair_rows = lax.broadcasted_iota(jnp.int32, (32, count), 0)
    side = (lax.broadcasted_iota(jnp.int32, (1, count), 1) >> 6) & 1
    counted = jnp.zeros((32, 1), jnp.float32)
    grids = []
    for panel in range(PANELS):
        pivot = pivots[panel:panel + 1, :]
        hits = (pair_rows == ((pivot >> 10) & 15) + 16 * side).astype(jnp.float32)
        counted += jnp.sum(hits, axis=1, keepdims=True)
        grids.append(jnp.concatenate([pivot[:, i * LANES:(i + 1) * LANES] for i in range(pieces)], axis=0))
    extra[0] = (jnp.max(counted).astype(jnp.int32) - 1) // CAP

    left = lax.broadcasted_iota(jnp.int32, grids[0].shape, 1) < LANES // 2
    lows = jnp.where(left, grids[0], pltpu.roll(grids[1], LANES // 2, axis=1))
    highs = jnp.where(left, pltpu.roll(grids[0], LANES // 2, axis=1), grids[1])
    own = jnp.where(core == 0, lows, highs)
    pivot = spread_row(own)
    chunk_hot = one_hot(lax.broadcasted_iota(jnp.int32, (chunks, count), 0) == (pivot >> 7))
    lane_hits = lax.broadcasted_iota(jnp.int32, (LANES, count), 0) == (pivot & (LANES - 1))
    flags = dot(chunk_hot, one_hot(lane_hits), NT).astype(jnp.bfloat16)
    here = lax.broadcasted_iota(jnp.int32, (chunks, chunks), 0)
    other = lax.broadcasted_iota(jnp.int32, (chunks, chunks), 1)
    block, other_block = here >> 3, other >> 3
    earlier = one_hot(((block == other_block) & (other < here)) | (block == other_block + 16))
    totals = dot(flags, jnp.ones((LANES, LANES), jnp.bfloat16), NN).astype(jnp.bfloat16)
    table = dot(flags, strictly_before(LANES), NN) + dot(earlier, totals, NN)
    high = jnp.floor(table * (1.0 / 128.0))
    parts = jnp.concatenate([high, table - 128.0 * high], axis=1).astype(jnp.bfloat16)
    found = dot(parts, chunk_hot, TN)
    found = 128.0 * found[:LANES] + found[LANES:]
    rank = jnp.sum(jnp.where(lane_hits, found, 0.0), axis=0, keepdims=True).astype(jnp.int32)
    rank = jnp.concatenate([rank[:, i * LANES:(i + 1) * LANES] for i in range(pieces)], axis=0)
    slot = ((own >> 10) & 15) * CAP + rank
    ranks[...] = rank
    slots[...] = slot
    firsts[...] = jnp.where(rank < CAP, slot, -1)


def reduce_kernel(first_row, spread, where, placed, panel_in, out, values, panel, come):
    quarter = panel.shape[0] // 4
    reads = [pltpu.make_async_copy(placed.at[pl.ds(first_row, LIVE_DEV)], values, come.at[0])]
    for part in range(4):
        rows = pl.ds(part * quarter, quarter)
        reads.append(pltpu.make_async_copy(panel_in.at[rows], panel.at[rows], come.at[part + 1]))
    for read in reads:
        read.start()
    slot_count = spread.shape[0]
    depth = 2 * LANES
    packed = spread[:, first_row:first_row + LIVE_DEV].astype(jnp.int32).astype(jnp.float32).astype(jnp.bfloat16)
    slot_lanes = lax.broadcasted_iota(jnp.int32, (depth, slot_count), 1)
    square = (LANES, LANES)
    diagonal = lax.broadcasted_iota(jnp.int32, square, 0) == lax.broadcasted_iota(jnp.int32, square, 1)
    turned = []
    for block in range(panel.shape[0] // depth):
        columns = [
            jnp.sum(
                jnp.where(diagonal, where[piece:piece + 1, :].astype(jnp.float32), 0.0), axis=1, keepdims=True
            )
            for piece in (2 * block, 2 * block + 1)
        ]
        here = jnp.concatenate(columns, axis=0).astype(jnp.int32)
        turned.append(jnp.transpose(dot(one_hot(slot_lanes == here), packed, NN).astype(jnp.bfloat16)))
    factors = jnp.concatenate(turned, axis=1)
    step = panel.shape[1] // 4
    for read in reads:
        read.wait()
    for part in range(4):
        cols = slice(part * step, (part + 1) * step)
        product = dot(factors, panel[:, cols], NN)
        out[:, cols] = remainder(values[:, cols].astype(jnp.float32) - product).astype(jnp.bfloat16)


def combine_kernel(own, incoming, out, result, done):
    step = LIVE_DEV // done.shape[0]
    writes = []
    for part in range(done.shape[0]):
        rows = slice(part * step, (part + 1) * step)
        total = own[rows, :].astype(jnp.float32) + incoming[rows, :].astype(jnp.float32)
        result[rows, :] = jnp.where(total >= modulus, total - modulus, total).astype(jnp.int32)
        write = pltpu.make_async_copy(result.at[pl.ds(part * step, step)], out.at[pl.ds(part * step, step)], done.at[part])
        write.start()
        writes.append(write)
    for write in writes:
        write.wait()


VMEM = pl.BlockSpec(memory_space=pltpu.VMEM)
SMEM = pl.BlockSpec(memory_space=pltpu.SMEM)
ANY = pl.BlockSpec(memory_space=pl.ANY)


def front(counts, pivots, rows, reducers, chips):
    capacity, width = rows.shape
    packed = jax.ShapeDtypeStruct((CAP, capacity), jnp.int16)
    return pl.pallas_call(
        front_kernel,
        out_shape=(
            jax.ShapeDtypeStruct((chips, *reducers.shape), jnp.bfloat16),
            jax.ShapeDtypeStruct((capacity, width), jnp.bfloat16),
            packed,
            packed,
            jax.ShapeDtypeStruct((2, width), jnp.float32),
        ),
        in_specs=[SMEM, VMEM, VMEM, VMEM],
        out_specs=(ANY, VMEM, VMEM, VMEM, VMEM),
        scratch_shapes=[
            pltpu.VMEM(reducers.shape, jnp.bfloat16),
            pltpu.SemaphoreType.DMA((chips,)),
        ],
        name="front",
    )(counts, pivots, rows, reducers)


def ranks(pivots):
    grid = jax.ShapeDtypeStruct((pivots.shape[1] // LANES, LANES), jnp.int32)
    return pl.pallas_call(
        ranks_kernel,
        out_shape=(grid, grid, grid, jax.ShapeDtypeStruct((1,), jnp.int32)),
        in_specs=[VMEM],
        out_specs=(VMEM, VMEM, VMEM, SMEM),
        name="ranks",
        compiler_params=pltpu.CompilerParams(vmem_limit_bytes=16 << 20),
        cost_estimate=pl.CostEstimate(flops=2_000_000_000, bytes_accessed=1_000_000, transcendentals=0),
    )(pivots)


def reduced(first_row, spread, where, placed, panel):
    width = panel.shape[1]
    return pl.pallas_call(
        functools.partial(reduce_kernel, first_row),
        out_shape=jax.ShapeDtypeStruct((LIVE_DEV, width), jnp.bfloat16),
        in_specs=[VMEM, VMEM, ANY, ANY],
        out_specs=VMEM,
        scratch_shapes=[
            pltpu.VMEM((LIVE_DEV, width), jnp.bfloat16),
            pltpu.VMEM(panel.shape, jnp.bfloat16),
            pltpu.SemaphoreType.DMA((5,)),
        ],
        compiler_params=pltpu.CompilerParams(vmem_limit_bytes=24 << 20),
        cost_estimate=pl.CostEstimate(flops=1_350_000_000, bytes_accessed=4_000_000, transcendentals=0),
    )(spread, where, placed, panel)


def combine(own, incoming):
    return pl.pallas_call(
        combine_kernel,
        out_shape=jax.ShapeDtypeStruct(own.shape, jnp.int32),
        in_specs=[VMEM] * 2,
        out_specs=pl.BlockSpec(memory_space=pltpu.HBM),
        scratch_shapes=[pltpu.VMEM(own.shape, jnp.int32), pltpu.SemaphoreType.DMA((4,))],
        name="combine",
        compiler_params=pltpu.CompilerParams(vmem_limit_bytes=8 << 20),
    )(own, incoming)


def shards(pair_rows, reducers, pivots, counts):
    chips = lax.axis_size(CHIP)
    col_width = pair_rows.shape[1]
    rows_dev = PANELS * reducers.shape[1]
    half = chips * rows_dev
    blocks = (counts, pivots, pair_rows, reducers.reshape(rows_dev, col_width))
    copies, placed, keep, send, columns = front(*blocks, chips)
    my_rank, my_slot, firsts, extra = ranks(pivots)

    def gather(keep, send):
        both = keep + swap(send, "core")
        both = both + swap(both, "yl")
        return lax.all_gather(both, "z", axis=0, tiled=True)

    def unpack(spread, where):
        table = (where.reshape(-1, 1) == lax.iota(jnp.int32, spread.shape[0])[None, :]).astype(jnp.bfloat16)
        return dot(table, spread.astype(jnp.bfloat16), NN).astype(jnp.bfloat16)

    panel = lax.all_to_all(copies, CHIP, 0, 0, tiled=True).reshape(half, col_width)
    spread = gather(keep, send)

    incoming = swap(reduced(LIVE_DEV, spread, firsts, placed, panel), "core")
    own = reduced(0, spread, firsts, placed, panel)
    first = combine(own, incoming)

    def another(state):
        step, result = state
        base = step * CAP
        want = (lax.iota(jnp.int32, CAP) + base).astype(jnp.float32)
        keep, send = [
            centered(dot((columns[side] == want[:, None]).astype(jnp.bfloat16), placed, NT)).astype(jnp.int16)
            for side in range(2)
        ]
        where = jnp.where((my_rank >= base) & (my_rank < base + CAP), my_slot - base, -1)
        factors = unpack(gather(keep, jnp.roll(send, LIVE_DEV, axis=1)), where)
        products = remainder(dot(factors, panel, TN))
        incoming = swap(products[LIVE_DEV:].astype(jnp.bfloat16), "core").astype(jnp.float32)
        result = result.astype(jnp.float32) - products[:LIVE_DEV] - incoming
        return step - 1, remainder(result).astype(jnp.int32)

    _, result = lax.while_loop(lambda state: state[0] > 0, another, (extra[0], first))
    return result


def solution(mesh):
    fine = Mesh(mesh.devices.reshape(2, 4, 2, 2, 16), (*ROW, *COL))
    return jax.shard_map(
        shards,
        mesh=fine,
        in_specs=(P(ROW, COL), P(None, ROW, COL), P(), P()),
        out_specs=P(ROW, COL),
        check_vma=False,
    )
```
